32 devices in a mesh: ms: 2 (over x), date: 4 (over y, core), pix: 4 (over z).
Axes of the slice: x: 2, y: 2, z: 4, core: 2. Of those that a mesh axis runs over, the one named last changes fastest.
Arguments:
- slc_stack: float32 [2, 64, 128, 128], P(None, ('ms', 'date'), 'pix'), may hold values from -6 to 6
Outputs:
- linked_phases: float32 [2, 64, 128, 128], P(None, ('ms', 'date'), 'pix')
- compressed_slc: float32 [2, 2, 128, 128], P(None, 'ms', 'pix', 'date')
The draws below stay inside these ranges and needn't reach their ends.
All inputs are finite; a program needn't handle non-finite values.
Results may differ from the reference program's by a relative error of at most 0.0001.
Values sent between devices are 32-bit elements; how exact they have to be, the bound alone decides.
No kernel may reach another device: no remote copies, remote signals or barrier semaphores. Data moves between devices by JAX's collectives and lax.ppermute only.
A program may use at most 128 MiB of HBM per device.

```python
import math
import jax
import jax.numpy as jnp
from jax import lax

M = 32
HALF = 5
ITERS = 3
WIN = 1
ROWS = 128
COLS = 128
STACK = 64
N_MS = 2


def levels(stream_key, shape, cuts, least, top_value):
    def one(axis_at, blocks):
        draws = jax.random.uniform(jax.random.fold_in(jax.random.fold_in(stream_key, 6), axis_at), (blocks,), jnp.float32, least / len(cuts), top_value / len(cuts))
        return jnp.repeat(jnp.exp(draws), shape[axis_at] // blocks).reshape((-1,) + (1,) * (len(shape) - axis_at - 1))

    factor_of = one(*cuts[0])
    for cut in cuts[1:]:
        factor_of = factor_of * one(*cut)
    return factor_of


def noise(own_key, dims, width, most, cuts=(), kind=jnp.bfloat16):
    drawn = jax.random.normal(own_key, dims, jnp.float32) * width
    if len(cuts) > 0:
        drawn = levels(own_key, dims, cuts, -0.22, 0.18) * drawn
    return jnp.clip(drawn, min=-most, max=most).astype(kind)


def setup_inputs(seed: int = 0) -> dict:
    splits = jax.random.split(jax.random.key(seed), 2)
    slc_stack = noise(splits[0], (2, STACK, ROWS, COLS), 1.0, 6.0, ((1, 8), (2, 4)), jnp.float32)
    return {"slc_stack": slc_stack}


epsilon = 1e-06
band_rows = 4

def window_area():
    return float((2 * HALF + 1) ** 2)

def box_sum(values, row_count, col_count):
    window_width = 2 * HALF + 1
    running = values[..., 0:row_count, :]
    for offset in range(1, window_width):
        running = running + values[..., offset:offset + row_count, :]
    summed = running[..., 0:col_count]
    for offset in range(1, window_width):
        summed = summed + running[..., offset:offset + col_count]
    return summed.reshape(summed.shape[:-2] + (row_count * col_count,))

def cross_sums(left_data, right_data, row_count, col_count):
    left_real = left_data[0][:, None]
    left_imag = left_data[1][:, None]
    right_real = right_data[0][None]
    right_imag = right_data[1][None]
    real_part = box_sum(left_real * right_real + left_imag * right_imag, row_count, col_count)
    imag_part = box_sum(left_imag * right_real - left_real * right_imag, row_count, col_count)
    return (real_part, imag_part)

def inverse_amplitude(data, row_count, col_count):
    energy = box_sum(data[0] * data[0] + data[1] * data[1], row_count, col_count)
    return lax.rsqrt(energy / window_area() + epsilon)

def coherence(real_part, imag_part, left_scale, right_scale):
    factor = left_scale[:, None] * right_scale[None] / window_area()
    return (real_part * factor, imag_part * factor)

def apply_matrix(matrix, vector):
    highest = lax.Precision.HIGHEST
    new_real = jnp.einsum('ijp,jp->ip', matrix[0], vector[0], precision=highest) - jnp.einsum('ijp,jp->ip', matrix[1], vector[1], precision=highest)
    new_imag = jnp.einsum('ijp,jp->ip', matrix[0], vector[1], precision=highest) + jnp.einsum('ijp,jp->ip', matrix[1], vector[0], precision=highest)
    return (new_real, new_imag)

def apply_adjoint(matrix, vector):
    highest = lax.Precision.HIGHEST
    new_real = jnp.einsum('jip,jp->ip', matrix[0], vector[0], precision=highest) + jnp.einsum('jip,jp->ip', matrix[1], vector[1], precision=highest)
    new_imag = jnp.einsum('jip,jp->ip', matrix[0], vector[1], precision=highest) - jnp.einsum('jip,jp->ip', matrix[1], vector[0], precision=highest)
    return (new_real, new_imag)

def link_own(row_band, row_count, col_count):
    date_count = row_band.shape[1]
    real_part, imag_part = cross_sums(row_band, row_band, row_count, col_count)
    scale_own = inverse_amplitude(row_band, row_count, col_count)
    matrix = coherence(real_part, imag_part, scale_own, scale_own)
    vec_real = jnp.ones(scale_own.shape, jnp.float32)
    vec_imag = jnp.zeros(scale_own.shape, jnp.float32)
    for repeat in range(ITERS):
        new_real, new_imag = apply_matrix(matrix, (vec_real, vec_imag))
        mean_square = lax.optimization_barrier(jnp.sum(new_real * new_real + new_imag * new_imag, axis=0)) / date_count
        factor = lax.rsqrt(mean_square + epsilon)
        vec_real = new_real * factor
        vec_imag = new_imag * factor
    centre = row_band[:, :, HALF:HALF + row_count, HALF:HALF + col_count].reshape(2, date_count, row_count * col_count)
    root = math.sqrt(date_count)
    comp_real = lax.optimization_barrier(jnp.sum(vec_real * centre[0] + vec_imag * centre[1], axis=0)) / root
    comp_imag = lax.optimization_barrier(jnp.sum(vec_real * centre[1] - vec_imag * centre[0], axis=0)) / root
    return jnp.stack([comp_real, comp_imag])

def link_window(row_band, slot_band, row_count, col_count):
    date_count = row_band.shape[1]
    slot_count = slot_band.shape[1]
    scale_own = inverse_amplitude(row_band, row_count, col_count)
    scale_slot = inverse_amplitude(slot_band, row_count, col_count)
    own_real, own_imag = cross_sums(row_band, row_band, row_count, col_count)
    own_matrix = coherence(own_real, own_imag, scale_own, scale_own)
    slot_real, slot_imag = cross_sums(slot_band, slot_band, row_count, col_count)
    slot_matrix = coherence(slot_real, slot_imag, scale_slot, scale_slot)
    mixed_real, mixed_imag = cross_sums(slot_band, row_band, row_count, col_count)
    mixed_matrix = coherence(mixed_real, mixed_imag, scale_slot, scale_own)
    slot_vec = (jnp.ones(scale_slot.shape, jnp.float32), jnp.zeros(scale_slot.shape, jnp.float32))
    own_vec = (jnp.ones(scale_own.shape, jnp.float32), jnp.zeros(scale_own.shape, jnp.float32))
    for repeat in range(ITERS):
        first_term = apply_matrix(slot_matrix, slot_vec)
        second_term = apply_matrix(mixed_matrix, own_vec)
        third_term = apply_adjoint(mixed_matrix, slot_vec)
        fourth_term = apply_matrix(own_matrix, own_vec)
        slot_new = (first_term[0] + second_term[0], first_term[1] + second_term[1])
        own_new = (third_term[0] + fourth_term[0], third_term[1] + fourth_term[1])
        mean_square = (lax.optimization_barrier(jnp.sum(slot_new[0] * slot_new[0] + slot_new[1] * slot_new[1], axis=0)) + lax.optimization_barrier(jnp.sum(own_new[0] * own_new[0] + own_new[1] * own_new[1], axis=0))) / (slot_count + date_count)
        factor = lax.rsqrt(mean_square + epsilon)
        slot_vec = (slot_new[0] * factor, slot_new[1] * factor)
        own_vec = (own_new[0] * factor, own_new[1] * factor)
    return jnp.stack([own_vec[0], own_vec[1]])

def reference(slc_stack):
    row_total = slc_stack.shape[2]
    col_total = slc_stack.shape[3]
    band_count = row_total // band_rows
    positions = jnp.arange(band_count, dtype=jnp.int32)
    widths = ((0, 0), (0, 0), (HALF, HALF), (HALF, HALF))
    compressed_images = []
    for ministack in range(N_MS):
        padded = jnp.pad(slc_stack[:, ministack * M:(ministack + 1) * M], widths)

        def first_band(position, padded=padded):
            row_band = lax.dynamic_slice_in_dim(padded, position * band_rows, band_rows + 2 * HALF, 2)
            return link_own(row_band, band_rows, col_total)
        pieces = lax.map(first_band, positions)
        compressed_images.append(pieces.reshape(band_count, 2, band_rows, col_total).transpose(1, 0, 2, 3).reshape(2, row_total, col_total))
    linked = []
    for ministack in range(N_MS):
        earlier = []
        for shift_by in range(1, WIN + 1):
            if ministack >= shift_by:
                earlier.append(compressed_images[ministack - shift_by])
            else:
                earlier.append(jnp.zeros((2, row_total, col_total), jnp.float32))
        padded = jnp.pad(slc_stack[:, ministack * M:(ministack + 1) * M], widths)
        slot_padded = jnp.pad(jnp.stack(earlier, axis=1), widths)

        def second_band(position, padded=padded, slot_padded=slot_padded):
            start = position * band_rows
            row_band = lax.dynamic_slice_in_dim(padded, start, band_rows + 2 * HALF, 2)
            slot_band = lax.dynamic_slice_in_dim(slot_padded, start, band_rows + 2 * HALF, 2)
            return link_window(row_band, slot_band, band_rows, col_total)
        pieces = lax.map(second_band, positions)
        linked.append(pieces.reshape(band_count, 2, M, band_rows, col_total).transpose(1, 2, 0, 3, 4).reshape(2, M, row_total, col_total))
    return (jnp.concatenate(linked, axis=1), jnp.stack(compressed_images, axis=1))
```

```python
import functools
import math

import jax
import jax.numpy as jnp
from jax import lax
from jax.experimental import pallas as pl
from jax.experimental.pallas import tpu as pltpu
from jax.sharding import PartitionSpec as P

HALF = 5
ITERS = 3
WIDTH = 2 * HALF + 1
AREA = float(WIDTH**2)
EPSILON = 1e-06
SUB = 8
LANES = 128
F32 = jnp.float32
BF16 = jnp.bfloat16


def row_sums(values, count):
    suffix = [None] * WIDTH
    running = values[WIDTH - 1]
    suffix[WIDTH - 1] = running
    for row in range(WIDTH - 2, -1, -1):
        running = running + values[row]
        suffix[row] = running
    out = [suffix[0]]
    prefix = None
    for row in range(1, count):
        term = values[WIDTH - 1 + row]
        prefix = term if prefix is None else prefix + term
        out.append(suffix[row] + prefix)
    return out


def put_split(x_ref, row, chunk, value):
    high = value.astype(BF16)
    low = (value - high.astype(F32)).astype(BF16)
    total = x_ref.shape[1] // 2
    x_ref[pl.ds(row, value.shape[0]), pl.ds(chunk * LANES, LANES)] = high
    x_ref[pl.ds(row, value.shape[0]), pl.ds(total + chunk * LANES, LANES)] = low


def products(x_ref, a_ref, other, rows):
    chunks, dates = a_ref.shape[2], a_ref.shape[3]
    for chunk in range(chunks):
        for first in range(0, dates, SUB):
            at = pl.ds(first, SUB)
            real, imag = [], []
            for row in range(rows + 2 * HALF):
                left_real, left_imag = a_ref[row, 0, chunk, at, :], a_ref[row, 1, chunk, at, :]
                right_real, right_imag = other(row, chunk)
                real.append(left_real * right_real + left_imag * right_imag)
                imag.append(left_imag * right_real - left_real * right_imag)
            for c, values in enumerate((real, imag)):
                for row, total in enumerate(row_sums(values, rows)):
                    put_split(x_ref, (row * 2 + c) * dates + first, chunk, total)


def energies(x_ref, a_ref, rows):
    chunks, dates = a_ref.shape[2], a_ref.shape[3]
    for chunk in range(chunks):
        for first in range(0, dates, SUB):
            at = pl.ds(first, SUB)
            values = []
            for row in range(rows + 2 * HALF):
                real, imag = a_ref[row, 0, chunk, at, :], a_ref[row, 1, chunk, at, :]
                values.append(real * real + imag * imag)
            for row, total in enumerate(row_sums(values, rows)):
                put_split(x_ref, row * dates + first, chunk, total)


def across(x_ref, size, band_ref, chunk):
    band = band_ref[:, pl.ds(chunk * LANES, LANES)]
    return jnp.dot(x_ref[0:size, :], band, preferred_element_type=F32)


def matvec(s_ref, v_ref, row, chunk, dates):
    blocks = dates // SUB
    real, imag = [None] * blocks, [None] * blocks
    for q in range(dates):
        v_real, v_imag = v_ref[0, pl.ds(q, 1), :], v_ref[1, pl.ds(q, 1), :]
        for b in range(blocks):
            s_real = s_ref[q, row, chunk, 0, pl.ds(b * SUB, SUB), :]
            s_imag = s_ref[q, row, chunk, 1, pl.ds(b * SUB, SUB), :]
            new_real = s_real * v_real - s_imag * v_imag
            new_imag = s_real * v_imag + s_imag * v_real
            real[b] = new_real if real[b] is None else real[b] + new_real
            imag[b] = new_imag if imag[b] is None else imag[b] + new_imag
    return jnp.concatenate(real, 0), jnp.concatenate(imag, 0)


def total_square(real, imag):
    return jnp.sum(real * real + imag * imag, axis=0, keepdims=True)


def each_row(rows, chunks, one_row):
    for chunk in range(chunks):
        lax.fori_loop(0, rows, functools.partial(one_row, chunk), 0)


def own_kernel(a_ref, band_ref, s_ref, r_ref, w_ref, comp_ref, x_ref, v_ref):
    rows, chunks, dates, _ = r_ref.shape

    energies(x_ref, a_ref, rows)
    for chunk in range(chunks):
        power = across(x_ref, rows * dates, band_ref, chunk)
        scale = lax.rsqrt(power / AREA + EPSILON)
        r_ref[:, chunk] = scale.reshape(rows, dates, LANES)

    def one_date(q, carry):
        def other(row, chunk):
            return a_ref[row, 0, chunk, pl.ds(q, 1), :], a_ref[row, 1, chunk, pl.ds(q, 1), :]

        products(x_ref, a_ref, other, rows)
        for chunk in range(chunks):
            summed = across(x_ref, rows * 2 * dates, band_ref, chunk)
            s_ref[q, :, chunk] = summed.reshape(rows, 2, dates, LANES)
        return carry

    lax.fori_loop(0, dates, one_date, 0)

    def one_row(chunk, row, carry):
        scale = r_ref[row, chunk]
        v_ref[0] = scale
        v_ref[1] = jnp.zeros_like(scale)
        for repeat in range(ITERS):
            real, imag = matvec(s_ref, v_ref, row, chunk, dates)
            real, imag = real * (scale / AREA), imag * (scale / AREA)
            if repeat == 0:
                w_ref[row, chunk, 0] = real
                w_ref[row, chunk, 1] = imag
            factor = lax.rsqrt(total_square(real, imag) / dates + EPSILON)
            real, imag = real * factor, imag * factor
            if repeat < ITERS - 1:
                v_ref[0] = real * scale
                v_ref[1] = imag * scale
        centre_real, centre_imag = a_ref[row + HALF, 0, chunk], a_ref[row + HALF, 1, chunk]
        root = math.sqrt(dates)
        comp_real = jnp.sum(real * centre_real + imag * centre_imag, axis=0, keepdims=True)
        comp_imag = jnp.sum(real * centre_imag - imag * centre_real, axis=0, keepdims=True)
        comp_ref[0, chunk, pl.ds(row, 1), :] = comp_real / root
        comp_ref[1, chunk, pl.ds(row, 1), :] = comp_imag / root
        return carry

    each_row(rows, chunks, one_row)


def window_kernel(
    slots, a_ref, z_ref, band_ref, s_ref, r_ref, w_ref, out_ref, x_ref, m_ref, zz_ref, rz_ref, v_ref, vz_ref
):
    rows, chunks, dates, _ = r_ref.shape

    energies(x_ref, z_ref, rows)
    for chunk in range(chunks):
        power = across(x_ref, rows * SUB, band_ref, chunk)
        rz_ref[:, chunk] = lax.rsqrt(power / AREA + EPSILON).reshape(rows, SUB, LANES)
    for slot in range(slots):

        def other(row, chunk, slot=slot):
            return z_ref[row, 0, chunk, pl.ds(slot, 1), :], z_ref[row, 1, chunk, pl.ds(slot, 1), :]

        products(x_ref, a_ref, other, rows)
        for chunk in range(chunks):
            summed = across(x_ref, rows * 2 * dates, band_ref, chunk)
            m_ref[slot, :, chunk] = summed.reshape(rows, 2, dates, LANES)
        products(x_ref, z_ref, other, rows)
        for chunk in range(chunks):
            summed = across(x_ref, rows * 2 * SUB, band_ref, chunk)
            zz_ref[slot, :, chunk] = summed.reshape(rows, 2, SUB, LANES)

    place = lax.broadcasted_iota(jnp.int32, (SUB, LANES), 0)

    def one_row(chunk, row, carry):
        scale = r_ref[row, chunk]
        scale_z = rz_ref[row, chunk]
        v_ref[0] = scale
        v_ref[1] = jnp.zeros_like(scale)
        vz_ref[0] = scale_z
        vz_ref[1] = jnp.zeros_like(scale_z)
        for repeat in range(ITERS):
            if repeat == 0:
                real, imag = w_ref[row, chunk, 0], w_ref[row, chunk, 1]
            else:
                real, imag = matvec(s_ref, v_ref, row, chunk, dates)
                real, imag = real * (scale / AREA), imag * (scale / AREA)
            add_real, add_imag = jnp.zeros_like(real), jnp.zeros_like(imag)
            z_real, z_imag = jnp.zeros_like(scale_z), jnp.zeros_like(scale_z)
            old_real, old_imag = v_ref[0], v_ref[1]
            for slot in range(slots):
                v_real, v_imag = vz_ref[0, pl.ds(slot, 1), :], vz_ref[1, pl.ds(slot, 1), :]
                m_real, m_imag = m_ref[slot, row, chunk, 0], m_ref[slot, row, chunk, 1]
                add_real = add_real + m_real * v_real - m_imag * v_imag
                add_imag = add_imag + m_real * v_imag + m_imag * v_real
                sum_real = jnp.sum(m_real * old_real + m_imag * old_imag, axis=0, keepdims=True)
                sum_imag = jnp.sum(m_real * old_imag - m_imag * old_real, axis=0, keepdims=True)
                z_real = z_real + jnp.where(place == slot, sum_real, 0.0)
                z_imag = z_imag + jnp.where(place == slot, sum_imag, 0.0)
                zz_real, zz_imag = zz_ref[slot, row, chunk, 0], zz_ref[slot, row, chunk, 1]
                z_real = z_real + zz_real * v_real - zz_imag * v_imag
                z_imag = z_imag + zz_real * v_imag + zz_imag * v_real
            real = real + add_real * (scale / AREA)
            imag = imag + add_imag * (scale / AREA)
            z_real = jnp.where(place < slots, z_real * (scale_z / AREA), 0.0)
            z_imag = jnp.where(place < slots, z_imag * (scale_z / AREA), 0.0)
            square = total_square(real, imag) + total_square(z_real, z_imag)
            factor = lax.rsqrt(square / (slots + dates) + EPSILON)
            real, imag = real * factor, imag * factor
            if repeat < ITERS - 1:
                v_ref[0] = real * scale
                v_ref[1] = imag * scale
                vz_ref[0] = z_real * factor * scale_z
                vz_ref[1] = z_imag * factor * scale_z
        out_ref[row, chunk, 0] = real
        out_ref[row, chunk, 1] = imag
        return carry

    each_row(rows, chunks, one_row)


def vmem():
    return pl.BlockSpec(memory_space=pltpu.VMEM)


def params(limit=48):
    return pltpu.CompilerParams(vmem_limit_bytes=limit * 2**20)


def link_own(a, band):
    rows, chunks, dates = a.shape[0] - 2 * HALF, a.shape[2], a.shape[3]
    return pl.pallas_call(
        own_kernel,
        out_shape=(
            jax.ShapeDtypeStruct((dates, rows, chunks, 2, dates, LANES), F32),
            jax.ShapeDtypeStruct((rows, chunks, dates, LANES), F32),
            jax.ShapeDtypeStruct((rows, chunks, 2, dates, LANES), F32),
            jax.ShapeDtypeStruct((2, chunks, rows, LANES), F32),
        ),
        in_specs=[vmem()] * 2,
        out_specs=[vmem()] * 4,
        scratch_shapes=[
            pltpu.VMEM((rows * 2 * dates, band.shape[0]), BF16),
            pltpu.VMEM((2, dates, LANES), F32),
        ],
        compiler_params=params(),
        name="link_own",
    )(a, band)


def link_window(a, z, band, s, r, w, slots):
    rows, chunks, dates, _ = r.shape
    return pl.pallas_call(
        functools.partial(window_kernel, slots),
        out_shape=jax.ShapeDtypeStruct((rows, chunks, 2, dates, LANES), F32),
        in_specs=[vmem()] * 6,
        out_specs=vmem(),
        scratch_shapes=[
            pltpu.VMEM((rows * 2 * dates, band.shape[0]), BF16),
            pltpu.VMEM((slots, rows, chunks, 2, dates, LANES), F32),
            pltpu.VMEM((slots, rows, chunks, 2, SUB, LANES), F32),
            pltpu.VMEM((rows, chunks, SUB, LANES), F32),
            pltpu.VMEM((2, dates, LANES), F32),
            pltpu.VMEM((2, SUB, LANES), F32),
        ],
        compiler_params=params(),
        name="link_window",
    )(a, z, band, s, r, w)


def swap(value, step):
    count = lax.axis_size("date")
    return lax.ppermute(value, "date", [(i, i ^ step) for i in range(count)])


def gather_windows(x):
    count, slabs = lax.axis_size("date"), lax.axis_size("pix")
    me = lax.axis_index("date")
    lead = x.transpose(2, 0, 1, 3)
    rows = lead.shape[0] // count
    tall = rows + 2 * HALF
    direct = rows >= HALF and count > 1
    if direct:
        padded = jnp.pad(lead, ((HALF, HALF), (0, 0), (0, 0), (0, 0)))
    else:
        ups = [(k, k + 1) for k in range(slabs - 1)]
        downs = [(b, a) for a, b in ups]
        above = lax.ppermute(lead[-HALF:], "pix", ups)
        below = lax.ppermute(lead[:HALF], "pix", downs)
        padded = jnp.concatenate([above, lead, below], 0)

    def window(target):
        return lax.dynamic_slice_in_dim(padded, target * rows, tall, 0)

    parts = [window(me)] + [swap(window(me ^ step), step) for step in range(1, count)]
    whole = jnp.concatenate(parts, 2)
    if not direct:
        return whole
    edges = []
    for step in range(count):
        up_from = step
        down_from = (step + 1) % count
        pairs = []
        for k in range(slabs):
            if k + 1 < slabs:
                pairs.append((up_from * slabs + k, k + 1))
            if k > 0:
                pairs.append((down_from * slabs + k, (count - 1) * slabs + k - 1))
        sent = jnp.where(me == up_from, lead[-HALF:], lead[:HALF])
        edges.append(lax.ppermute(sent, ("date", "pix"), pairs))
    top = jnp.concatenate([edges[j] for j in range(count)], 2)
    last = count - 1
    bottom = jnp.concatenate([edges[((last ^ j) - 1) % count] for j in range(count)], 2)
    first_rows = jnp.where(me == 0, top, whole[:HALF])
    last_rows = jnp.where(me == last, bottom, whole[-HALF:])
    return jnp.concatenate([first_rows, whole[HALF:-HALF], last_rows], 0)


def earlier_windows(compressed, shift_by):
    stacks, count, slabs = lax.axis_size("ms"), lax.axis_size("date"), lax.axis_size("pix")
    rows = compressed.shape[1]
    reach = -(-HALF // rows)
    blocks = count * slabs

    def index(stack, block):
        k, d = divmod(block, count)
        return (stack * count + d) * slabs + k

    lead = compressed.transpose(1, 0, 2)
    parts = []
    for offset in range(-reach, reach + 1):
        low = max(0, -HALF - offset * rows)
        high = min(rows, rows + HALF - offset * rows)
        pairs = []
        for stack in range(stacks - shift_by):
            for block in range(blocks):
                target = block - offset
                if 0 <= target < blocks:
                    pairs.append((index(stack, block), index(stack + shift_by, target)))
        parts.append(lax.ppermute(lead[low:high], ("ms", "date", "pix"), pairs))
    return jnp.concatenate(parts, 0)


def body(slc_stack):
    count = lax.axis_size("date")
    me = lax.axis_index("date")
    a = gather_windows(slc_stack)
    cols = a.shape[3]
    chunks = cols // LANES
    a = a.reshape(a.shape[:3] + (chunks, LANES)).transpose(0, 1, 3, 2, 4)
    rows = a.shape[0] - 2 * HALF
    places = jnp.arange(cols, dtype=jnp.int32)
    band = (jnp.abs(places[:, None] - places[None, :]) <= HALF).astype(BF16)
    band = jnp.concatenate([band, band], 0)
    s, r, w, compressed = link_own(a, band)
    compressed = compressed.transpose(0, 2, 1, 3).reshape(2, rows, cols)
    slots = min(3, lax.axis_size("ms") - 1)
    z = jnp.stack([earlier_windows(compressed, shift_by) for shift_by in range(1, slots + 1)], 2)
    z = jnp.pad(z, ((0, 0), (0, 0), (0, SUB - slots), (0, 0)))
    z = z.reshape(z.shape[:3] + (chunks, LANES)).transpose(0, 1, 3, 2, 4)
    linked = link_window(a, z, band, s, r, w, slots)
    own = slc_stack.shape[1]
    sent = []
    for j in range(count):
        dates = linked[:, :, :, j * own : (j + 1) * own].transpose(2, 3, 0, 1, 4).reshape(2, own, rows, cols)
        sent.append(jnp.concatenate([dates, compressed[:, None]], 1))
    out = jnp.zeros((2, own + 1, rows * count, cols), F32)
    for step in range(count):
        piece = swap(sent[step], step) if step else sent[0]
        out = lax.dynamic_update_slice_in_dim(out, piece, (me ^ step) * rows, 2)
    width = cols // count
    mine = lax.dynamic_slice_in_dim(out[:, own:], me * width, width, 3)
    return (out[:, :own], mine)


def solution(mesh):
    in_specs = (P(None, ("ms", "date"), "pix", None),)
    out_specs = (P(None, ("ms", "date"), "pix", None), P(None, "ms", "pix", "date"))
    return jax.shard_map(body, mesh=mesh, in_specs=in_specs, out_specs=out_specs, check_vma=False)
```

```python
import functools
import math

import jax
import jax.numpy as jnp
from jax import lax
from jax.experimental import pallas as pl
from jax.experimental.pallas import tpu as pltpu
from jax.sharding import PartitionSpec as P

HALF = 5
ITERS = 3
WIDTH = 2 * HALF + 1
AREA = float(WIDTH**2)
EPSILON = 1e-06
SUB = 8
LANES = 128
F32 = jnp.float32
BF16 = jnp.bfloat16


def row_sums(values, count):
    suffix = [None] * WIDTH
    running = values[WIDTH - 1]
    suffix[WIDTH - 1] = running
    for row in range(WIDTH - 2, -1, -1):
        running = running + values[row]
        suffix[row] = running
    out = [suffix[0]]
    prefix = None
    for row in range(1, count):
        term = values[WIDTH - 1 + row]
        prefix = term if prefix is None else prefix + term
        out.append(suffix[row] + prefix)
    return out


def put_split(x_ref, at, chunk, value):
    high = value.astype(BF16)
    low = (value - high.astype(F32)).astype(BF16)
    total = x_ref.shape[1] // 2
    x_ref[pl.ds(at, value.shape[0]), pl.ds(chunk * LANES, LANES)] = high
    x_ref[pl.ds(at, value.shape[0]), pl.ds(total + chunk * LANES, LANES)] = low


def products(x_ref, blocks, other, rows, chunks):
    for chunk in range(chunks):
        for place, (ref, first) in enumerate(blocks):
            at = pl.ds(first, SUB)
            real, imag = [], []
            for row in range(rows + 2 * HALF):
                left_real, left_imag = ref[row, 0, chunk, at, :], ref[row, 1, chunk, at, :]
                right_real, right_imag = other(row, chunk)
                real.append(left_real * right_real + left_imag * right_imag)
                imag.append(left_imag * right_real - left_real * right_imag)
            sums = zip(row_sums(real, rows), row_sums(imag, rows))
            for row, both in enumerate(sums):
                put_split(x_ref, (row * len(blocks) + place) * 2 * SUB, chunk, jnp.concatenate(both, 0))


def energies(x_ref, ref, rows, chunks, dates):
    step = math.gcd(dates, 2 * SUB)
    for chunk in range(chunks):
        for first in range(0, dates, step):
            at = pl.ds(first, step)
            values = []
            for row in range(rows + 2 * HALF):
                real, imag = ref[row, 0, chunk, at, :], ref[row, 1, chunk, at, :]
                values.append(real * real + imag * imag)
            for row, total in enumerate(row_sums(values, rows)):
                put_split(x_ref, row * dates + first, chunk, total)


def across(x_ref, size, band_ref, chunk):
    band = band_ref[:, pl.ds(chunk * LANES, LANES)]
    return jnp.dot(x_ref[0:size, :], band, preferred_element_type=F32)


def spread(ref, *place):
    return ref[place[:-1] + (pl.ds(place[-1], SUB, stride=0), slice(None))]


def accumulate(total, term):
    return term if total is None else total + term


def matvec(s_ref, v_ref, base, dates):
    blocks = dates // SUB
    real, imag = [None] * blocks, [None] * blocks
    for q in range(dates):
        v_real, v_imag = spread(v_ref, 0, q), spread(v_ref, 1, q)
        for b in range(blocks):
            at = q * dates + b * SUB
            s_real = s_ref[pl.ds(base + at, SUB), :]
            s_imag = s_ref[pl.ds(base + dates * dates + at, SUB), :]
            real[b] = accumulate(real[b], s_real * v_real - s_imag * v_imag)
            imag[b] = accumulate(imag[b], s_real * v_imag + s_imag * v_real)
    return jnp.concatenate(real, 0), jnp.concatenate(imag, 0)


def fill_and_apply(s_ref, v_ref, base, dates):
    blocks = dates // SUB
    real, imag = [None] * blocks, [None] * blocks
    half = dates * dates
    for q in range(dates):
        v_real = spread(v_ref, 0, q)
        for b in range(blocks):
            at = pl.ds(base + q * dates + b * SUB, SUB)
            at_imag = pl.ds(base + half + q * dates + b * SUB, SUB)
            if b < q // SUB:
                turned = base + b * SUB * dates + q
                s_real = s_ref[pl.ds(turned, SUB, stride=dates), :]
                s_imag = -s_ref[pl.ds(turned + half, SUB, stride=dates), :]
                s_ref[at, :] = s_real
                s_ref[at_imag, :] = s_imag
            else:
                s_real, s_imag = s_ref[at, :], s_ref[at_imag, :]
            real[b] = accumulate(real[b], s_real * v_real)
            imag[b] = accumulate(imag[b], s_imag * v_real)
    return jnp.concatenate(real, 0), jnp.concatenate(imag, 0)


def total_square(real, imag):
    return jnp.sum(real * real + imag * imag, axis=0, keepdims=True)


def each_row(rows, chunks, one_row):
    for chunk in range(chunks):
        lax.fori_loop(0, rows, functools.partial(one_row, chunk), 0)


def own_kernel(a_ref, band_ref, s_ref, r_ref, w_ref, comp_ref, v_ref, *x_refs):
    rows, chunks, dates, _ = r_ref.shape
    blocks = dates // SUB
    half = dates * dates
    group = len(x_refs)

    energies(x_refs[0], a_ref, rows, chunks, dates)
    for chunk in range(chunks):
        power = across(x_refs[0], rows * dates, band_ref, chunk)
        scale = lax.rsqrt(power / AREA + EPSILON)
        r_ref[:, chunk] = scale.reshape(rows, dates, LANES)

    for q_block in range(blocks):
        kept = [(a_ref, b * SUB) for b in range(q_block, blocks)]

        def one_group(turn, carry, q_block=q_block, kept=kept):
            for u in range(group):
                q = q_block * SUB + turn * group + u

                def other(row, chunk, q=q):
                    return spread(a_ref, row, 0, chunk, q), spread(a_ref, row, 1, chunk, q)

                products(x_refs[u], kept, other, rows, chunks)
                for chunk in range(chunks):
                    summed = across(x_refs[u], rows * len(kept) * 2 * SUB, band_ref, chunk)
                    for row in range(rows):
                        for place, (_, first) in enumerate(kept):
                            for c in range(2):
                                value = summed[((row * len(kept) + place) * 2 + c) * SUB :][:SUB]
                                at = (row * chunks + chunk) * 2 * half + c * half + q * dates + first
                                s_ref[pl.ds(pl.multiple_of(at, SUB), SUB), :] = value
            return carry

        lax.fori_loop(0, SUB // group, one_group, 0)

    def one_row(chunk, row, carry):
        base = pl.multiple_of((row * chunks + chunk) * 2 * half, SUB)
        scale = r_ref[row, chunk]
        v_ref[0] = scale
        for repeat in range(ITERS):
            if repeat == 0:
                real, imag = fill_and_apply(s_ref, v_ref, base, dates)
            else:
                real, imag = matvec(s_ref, v_ref, base, dates)
            real, imag = real * (scale / AREA), imag * (scale / AREA)
            if repeat == 0:
                w_ref[row, chunk, 0] = real
                w_ref[row, chunk, 1] = imag
            factor = lax.rsqrt(total_square(real, imag) / dates + EPSILON)
            real, imag = real * factor, imag * factor
            if repeat < ITERS - 1:
                v_ref[0] = real * scale
                v_ref[1] = imag * scale
        centre_real, centre_imag = a_ref[row + HALF, 0, chunk], a_ref[row + HALF, 1, chunk]
        root = math.sqrt(dates)
        comp_real = jnp.sum(real * centre_real + imag * centre_imag, axis=0, keepdims=True)
        comp_imag = jnp.sum(real * centre_imag - imag * centre_real, axis=0, keepdims=True)
        comp_ref[0, chunk, pl.ds(row, 1), :] = comp_real / root
        comp_ref[1, chunk, pl.ds(row, 1), :] = comp_imag / root
        return carry

    each_row(rows, chunks, one_row)


def window_kernel(
    slots, a_ref, z_ref, band_ref, s_ref, r_ref, w_ref, out_ref, x_ref, m_ref, zz_ref, rz_ref, v_ref, vz_ref
):
    rows, chunks, dates, _ = r_ref.shape
    blocks = dates // SUB
    half = dates * dates

    energies(x_ref, z_ref, rows, chunks, SUB)
    for chunk in range(chunks):
        power = across(x_ref, rows * SUB, band_ref, chunk)
        rz_ref[:, chunk] = lax.rsqrt(power / AREA + EPSILON).reshape(rows, SUB, LANES)
    kept = [(a_ref, b * SUB) for b in range(blocks)] + [(z_ref, 0)]
    for slot in range(slots):

        def other(row, chunk, slot=slot):
            return spread(z_ref, row, 0, chunk, slot), spread(z_ref, row, 1, chunk, slot)

        products(x_ref, kept, other, rows, chunks)
        for chunk in range(chunks):
            summed = across(x_ref, rows * len(kept) * 2 * SUB, band_ref, chunk)
            for row in range(rows):
                for place, (_, first) in enumerate(kept):
                    for c in range(2):
                        value = summed[((row * len(kept) + place) * 2 + c) * SUB :][:SUB]
                        if place < blocks:
                            m_ref[slot, row, chunk, c, pl.ds(first, SUB), :] = value
                        else:
                            zz_ref[slot, row, chunk, c] = value

    place = lax.broadcasted_iota(jnp.int32, (SUB, LANES), 0)

    def one_row(chunk, row, carry):
        base = pl.multiple_of((row * chunks + chunk) * 2 * half, SUB)
        scale = r_ref[row, chunk]
        scale_z = rz_ref[row, chunk]
        v_ref[0] = scale
        v_ref[1] = jnp.zeros_like(scale)
        vz_ref[0] = scale_z
        vz_ref[1] = jnp.zeros_like(scale_z)
        for repeat in range(ITERS):
            if repeat == 0:
                real, imag = w_ref[row, chunk, 0], w_ref[row, chunk, 1]
            else:
                real, imag = matvec(s_ref, v_ref, base, dates)
                real, imag = real * (scale / AREA), imag * (scale / AREA)
            add_real, add_imag = jnp.zeros_like(real), jnp.zeros_like(imag)
            z_real, z_imag = jnp.zeros_like(scale_z), jnp.zeros_like(scale_z)
            old_real, old_imag = v_ref[0], v_ref[1]
            for slot in range(slots):
                v_real, v_imag = vz_ref[0, pl.ds(slot, 1), :], vz_ref[1, pl.ds(slot, 1), :]
                m_real, m_imag = m_ref[slot, row, chunk, 0], m_ref[slot, row, chunk, 1]
                add_real = add_real + m_real * v_real - m_imag * v_imag
                add_imag = add_imag + m_real * v_imag + m_imag * v_real
                sum_real = jnp.sum(m_real * old_real + m_imag * old_imag, axis=0, keepdims=True)
                sum_imag = jnp.sum(m_real * old_imag - m_imag * old_real, axis=0, keepdims=True)
                z_real = z_real + jnp.where(place == slot, sum_real, 0.0)
                z_imag = z_imag + jnp.where(place == slot, sum_imag, 0.0)
                zz_real, zz_imag = zz_ref[slot, row, chunk, 0], zz_ref[slot, row, chunk, 1]
                z_real = z_real + zz_real * v_real - zz_imag * v_imag
                z_imag = z_imag + zz_real * v_imag + zz_imag * v_real
            real = real + add_real * (scale / AREA)
            imag = imag + add_imag * (scale / AREA)
            z_real = jnp.where(place < slots, z_real * (scale_z / AREA), 0.0)
            z_imag = jnp.where(place < slots, z_imag * (scale_z / AREA), 0.0)
            square = total_square(real, imag) + total_square(z_real, z_imag)
            factor = lax.rsqrt(square / (slots + dates) + EPSILON)
            real, imag = real * factor, imag * factor
            if repeat < ITERS - 1:
                v_ref[0] = real * scale
                v_ref[1] = imag * scale
                vz_ref[0] = z_real * factor * scale_z
                vz_ref[1] = z_imag * factor * scale_z
        out_ref[row, chunk, 0] = real
        out_ref[row, chunk, 1] = imag
        return carry

    each_row(rows, chunks, one_row)


def vmem():
    return pl.BlockSpec(memory_space=pltpu.VMEM)


def params(limit=24):
    return pltpu.CompilerParams(vmem_limit_bytes=limit * 2**20)


def link_own(a, band, group=4):
    rows, chunks, dates = a.shape[0] - 2 * HALF, a.shape[2], a.shape[3]
    return pl.pallas_call(
        own_kernel,
        out_shape=(
            jax.ShapeDtypeStruct((rows * chunks * 2 * dates * dates, LANES), F32),
            jax.ShapeDtypeStruct((rows, chunks, dates, LANES), F32),
            jax.ShapeDtypeStruct((rows, chunks, 2, dates, LANES), F32),
            jax.ShapeDtypeStruct((2, chunks, rows, LANES), F32),
        ),
        in_specs=[vmem()] * 2,
        out_specs=[vmem()] * 4,
        scratch_shapes=[pltpu.VMEM((2, dates, LANES), F32)]
        + [pltpu.VMEM((rows * 2 * dates, band.shape[0]), BF16)] * group,
        compiler_params=params(),
        name="link_own",
    )(a, band)


def link_window(a, z, band, s, r, w, slots):
    rows, chunks, dates, _ = r.shape
    return pl.pallas_call(
        functools.partial(window_kernel, slots),
        out_shape=jax.ShapeDtypeStruct((rows, chunks, 2, dates, LANES), F32),
        in_specs=[vmem()] * 6,
        out_specs=vmem(),
        scratch_shapes=[
            pltpu.VMEM((rows * 2 * (dates + SUB), band.shape[0]), BF16),
            pltpu.VMEM((slots, rows, chunks, 2, dates, LANES), F32),
            pltpu.VMEM((slots, rows, chunks, 2, SUB, LANES), F32),
            pltpu.VMEM((rows, chunks, SUB, LANES), F32),
            pltpu.VMEM((2, dates, LANES), F32),
            pltpu.VMEM((2, SUB, LANES), F32),
        ],
        compiler_params=params(),
        name="link_window",
    )(a, z, band, s, r, w)


def swap(value, step):
    count = lax.axis_size("date")
    return lax.ppermute(value, "date", [(i, i ^ step) for i in range(count)])


def gather_windows(x):
    count, slabs = lax.axis_size("date"), lax.axis_size("pix")
    me = lax.axis_index("date")
    lead = x.transpose(2, 0, 1, 3)
    rows = lead.shape[0] // count
    tall = rows + 2 * HALF
    direct = rows >= HALF and count > 1
    if direct:
        padded = jnp.pad(lead, ((HALF, HALF), (0, 0), (0, 0), (0, 0)))
    else:
        ups = [(k, k + 1) for k in range(slabs - 1)]
        downs = [(b, a) for a, b in ups]
        above = lax.ppermute(lead[-HALF:], "pix", ups)
        below = lax.ppermute(lead[:HALF], "pix", downs)
        padded = jnp.concatenate([above, lead, below], 0)

    def window(target):
        return lax.dynamic_slice_in_dim(padded, target * rows, tall, 0)

    parts = [window(me)] + [swap(window(me ^ step), step) for step in range(1, count)]
    whole = jnp.concatenate(parts, 2)
    if not direct:
        return whole
    edges = []
    for step in range(count):
        up_from = step
        down_from = (step + 1) % count
        pairs = []
        for k in range(slabs):
            if k + 1 < slabs:
                pairs.append((up_from * slabs + k, k + 1))
            if k > 0:
                pairs.append((down_from * slabs + k, (count - 1) * slabs + k - 1))
        sent = jnp.where(me == up_from, lead[-HALF:], lead[:HALF])
        edges.append(lax.ppermute(sent, ("date", "pix"), pairs))
    top = jnp.concatenate([edges[j] for j in range(count)], 2)
    last = count - 1
    bottom = jnp.concatenate([edges[((last ^ j) - 1) % count] for j in range(count)], 2)
    first_rows = jnp.where(me == 0, top, whole[:HALF])
    last_rows = jnp.where(me == last, bottom, whole[-HALF:])
    return jnp.concatenate([first_rows, whole[HALF:-HALF], last_rows], 0)


def earlier_windows(compressed, shift_by):
    stacks, count, slabs = lax.axis_size("ms"), lax.axis_size("date"), lax.axis_size("pix")
    rows = compressed.shape[1]
    reach = -(-HALF // rows)
    blocks = count * slabs

    def index(stack, block):
        k, d = divmod(block, count)
        return (stack * count + d) * slabs + k

    lead = compressed.transpose(1, 0, 2)
    parts = []
    for offset in range(-reach, reach + 1):
        low = max(0, -HALF - offset * rows)
        high = min(rows, rows + HALF - offset * rows)
        pairs = []
        for stack in range(stacks - shift_by):
            for block in range(blocks):
                target = block - offset
                if 0 <= target < blocks:
                    pairs.append((index(stack, block), index(stack + shift_by, target)))
        parts.append(lax.ppermute(lead[low:high], ("ms", "date", "pix"), pairs))
    return jnp.concatenate(parts, 0)


def body(slc_stack):
    count = lax.axis_size("date")
    me = lax.axis_index("date")
    a = gather_windows(slc_stack)
    cols = a.shape[3]
    chunks = cols // LANES
    a = a.reshape(a.shape[:3] + (chunks, LANES)).transpose(0, 1, 3, 2, 4)
    rows = a.shape[0] - 2 * HALF
    places = jnp.arange(cols, dtype=jnp.int32)
    band = (jnp.abs(places[:, None] - places[None, :]) <= HALF).astype(BF16)
    band = jnp.concatenate([band, band], 0)
    s, r, w, compressed = link_own(a, band)
    compressed = compressed.transpose(0, 2, 1, 3).reshape(2, rows, cols)
    slots = min(3, lax.axis_size("ms") - 1)
    z = jnp.stack([earlier_windows(compressed, shift_by) for shift_by in range(1, slots + 1)], 2)
    z = jnp.pad(z, ((0, 0), (0, 0), (0, SUB - slots), (0, 0)))
    z = z.reshape(z.shape[:3] + (chunks, LANES)).transpose(0, 1, 3, 2, 4)
    linked = link_window(a, z, band, s, r, w, slots)
    own = slc_stack.shape[1]
    sent = []
    for j in range(count):
        dates = linked[:, :, :, j * own : (j + 1) * own].transpose(2, 3, 0, 1, 4).reshape(2, own, rows, cols)
        sent.append(jnp.concatenate([dates, compressed[:, None]], 1))
    out = jnp.zeros((2, own + 1, rows * count, cols), F32)
    for step in range(count):
        piece = swap(sent[step], step) if step else sent[0]
        out = lax.dynamic_update_slice_in_dim(out, piece, (me ^ step) * rows, 2)
    width = cols // count
    mine = lax.dynamic_slice_in_dim(out[:, own:], me * width, width, 3)
    return (out[:, :own], mine)


def solution(mesh):
    in_specs = (P(None, ("ms", "date"), "pix", None),)
    out_specs = (P(None, ("ms", "date"), "pix", None), P(None, "ms", "pix", "date"))
    return jax.shard_map(body, mesh=mesh, in_specs=in_specs, out_specs=out_specs, check_vma=False)
```

```python
import functools
import math

import jax
import jax.numpy as jnp
from jax import lax
from jax.experimental import pallas as pl
from jax.experimental.pallas import tpu as pltpu
from jax.sharding import PartitionSpec as P

HALF = 5
ITERS = 3
WIDTH = 2 * HALF + 1
AREA = float(WIDTH**2)
EPSILON = 1e-06
SUB = 8
LANES = 128
F32 = jnp.float32
BF16 = jnp.bfloat16


def row_sums(values, count):
    suffix = [None] * WIDTH
    running = values[WIDTH - 1]
    suffix[WIDTH - 1] = running
    for row in range(WIDTH - 2, -1, -1):
        running = running + values[row]
        suffix[row] = running
    out = [suffix[0]]
    prefix = None
    for row in range(1, count):
        term = values[WIDTH - 1 + row]
        prefix = term if prefix is None else prefix + term
        out.append(suffix[row] + prefix)
    return out


def put_split(x_ref, at, chunk, value):
    high = value.astype(BF16)
    low = (value - high.astype(F32)).astype(BF16)
    total = x_ref.shape[1] // 2
    x_ref[pl.ds(at, value.shape[0]), pl.ds(chunk * LANES, LANES)] = high
    x_ref[pl.ds(at, value.shape[0]), pl.ds(total + chunk * LANES, LANES)] = low


def products(x_ref, blocks, other, rows, chunks):
    for chunk in range(chunks):
        for place, (ref, first) in enumerate(blocks):
            at = pl.ds(first, SUB)
            real, imag = [], []
            for row in range(rows + 2 * HALF):
                left_real, left_imag = ref[row, 0, chunk, at, :], ref[row, 1, chunk, at, :]
                right_real, right_imag = other(row, chunk)
                real.append(left_real * right_real + left_imag * right_imag)
                imag.append(left_imag * right_real - left_real * right_imag)
            sums = zip(row_sums(real, rows), row_sums(imag, rows))
            for row, both in enumerate(sums):
                put_split(x_ref, (row * len(blocks) + place) * 2 * SUB, chunk, jnp.concatenate(both, 0))


def energies(x_ref, ref, rows, chunks, dates):
    step = math.gcd(dates, 2 * SUB)
    for chunk in range(chunks):
        for first in range(0, dates, step):
            at = pl.ds(first, step)
            values = []
            for row in range(rows + 2 * HALF):
                real, imag = ref[row, 0, chunk, at, :], ref[row, 1, chunk, at, :]
                values.append(real * real + imag * imag)
            for row, total in enumerate(row_sums(values, rows)):
                put_split(x_ref, row * dates + first, chunk, total)


def across(x_ref, size, band_ref, chunk):
    band = band_ref[:, pl.ds(chunk * LANES, LANES)]
    return jnp.dot(x_ref[0:size, :], band, preferred_element_type=F32)


def spread(ref, *place):
    return ref[place[:-1] + (pl.ds(place[-1], SUB, stride=0), slice(None))]


def accumulate(total, term):
    return term if total is None else total + term


def matvec(s_ref, v_ref, base, dates):
    blocks = dates // SUB
    real, imag = [None] * blocks, [None] * blocks
    for q in range(dates):
        v_real, v_imag = spread(v_ref, 0, q), spread(v_ref, 1, q)
        for b in range(blocks):
            at = q * dates + b * SUB
            s_real = s_ref[pl.ds(base + at, SUB), :]
            s_imag = s_ref[pl.ds(base + dates * dates + at, SUB), :]
            real[b] = accumulate(real[b], s_real * v_real - s_imag * v_imag)
            imag[b] = accumulate(imag[b], s_real * v_imag + s_imag * v_real)
    return jnp.concatenate(real, 0), jnp.concatenate(imag, 0)


def fill_and_apply(s_ref, v_ref, base, dates):
    blocks = dates // SUB
    real, imag = [None] * blocks, [None] * blocks
    half = dates * dates
    for q in range(dates):
        v_real = spread(v_ref, 0, q)
        for b in range(blocks):
            at = pl.ds(base + q * dates + b * SUB, SUB)
            at_imag = pl.ds(base + half + q * dates + b * SUB, SUB)
            if b < q // SUB:
                turned = base + b * SUB * dates + q
                s_real = s_ref[pl.ds(turned, SUB, stride=dates), :]
                s_imag = -s_ref[pl.ds(turned + half, SUB, stride=dates), :]
                s_ref[at, :] = s_real
                s_ref[at_imag, :] = s_imag
            else:
                s_real, s_imag = s_ref[at, :], s_ref[at_imag, :]
            real[b] = accumulate(real[b], s_real * v_real)
            imag[b] = accumulate(imag[b], s_imag * v_real)
    return jnp.concatenate(real, 0), jnp.concatenate(imag, 0)


def total_square(real, imag):
    return jnp.sum(real * real + imag * imag, axis=0, keepdims=True)


def each_row(rows, chunks, one_row):
    for chunk in range(chunks):
        lax.fori_loop(0, rows, functools.partial(one_row, chunk), 0)


def own_kernel(a_ref, band_ref, s_ref, r_ref, w_ref, comp_ref, v_ref, *x_refs):
    rows, chunks, dates, _ = r_ref.shape
    blocks = dates // SUB
    half = dates * dates
    group = len(x_refs)

    energies(x_refs[0], a_ref, rows, chunks, dates)
    for chunk in range(chunks):
        power = across(x_refs[0], rows * dates, band_ref, chunk)
        scale = lax.rsqrt(power / AREA + EPSILON)
        r_ref[:, chunk] = scale.reshape(rows, dates, LANES)

    for q_block in range(blocks):
        kept = [(a_ref, b * SUB) for b in range(q_block, blocks)]

        def one_group(turn, carry, q_block=q_block, kept=kept):
            for u in range(group):
                q = q_block * SUB + turn * group + u

                def other(row, chunk, q=q):
                    return spread(a_ref, row, 0, chunk, q), spread(a_ref, row, 1, chunk, q)

                products(x_refs[u], kept, other, rows, chunks)
                for chunk in range(chunks):
                    summed = across(x_refs[u], rows * len(kept) * 2 * SUB, band_ref, chunk)
                    for row in range(rows):
                        for place, (_, first) in enumerate(kept):
                            for c in range(2):
                                value = summed[((row * len(kept) + place) * 2 + c) * SUB :][:SUB]
                                at = (row * chunks + chunk) * 2 * half + c * half + q * dates + first
                                s_ref[pl.ds(pl.multiple_of(at, SUB), SUB), :] = value
            return carry

        lax.fori_loop(0, SUB // group, one_group, 0)

    def one_row(chunk, row, carry):
        base = pl.multiple_of((row * chunks + chunk) * 2 * half, SUB)
        scale = r_ref[row, chunk]
        v_ref[0] = scale
        for repeat in range(ITERS):
            if repeat == 0:
                real, imag = fill_and_apply(s_ref, v_ref, base, dates)
            else:
                real, imag = matvec(s_ref, v_ref, base, dates)
            real, imag = real * (scale / AREA), imag * (scale / AREA)
            if repeat == 0:
                w_ref[row, chunk, 0] = real
                w_ref[row, chunk, 1] = imag
            factor = lax.rsqrt(total_square(real, imag) / dates + EPSILON)
            real, imag = real * factor, imag * factor
            if repeat < ITERS - 1:
                v_ref[0] = real * scale
                v_ref[1] = imag * scale
        centre_real, centre_imag = a_ref[row + HALF, 0, chunk], a_ref[row + HALF, 1, chunk]
        root = math.sqrt(dates)
        comp_real = jnp.sum(real * centre_real + imag * centre_imag, axis=0, keepdims=True)
        comp_imag = jnp.sum(real * centre_imag - imag * centre_real, axis=0, keepdims=True)
        comp_ref[0, chunk, pl.ds(row, 1), :] = comp_real / root
        comp_ref[1, chunk, pl.ds(row, 1), :] = comp_imag / root
        return carry

    each_row(rows, chunks, one_row)


def window_kernel(
    slots, a_ref, z_ref, band_ref, s_ref, r_ref, w_ref, out_ref, x_ref, m_ref, zz_ref, rz_ref, v_ref, vz_ref
):
    rows, chunks, dates, _ = r_ref.shape
    blocks = dates // SUB
    half = dates * dates

    energies(x_ref, z_ref, rows, chunks, SUB)
    for chunk in range(chunks):
        power = across(x_ref, rows * SUB, band_ref, chunk)
        rz_ref[:, chunk] = lax.rsqrt(power / AREA + EPSILON).reshape(rows, SUB, LANES)
    kept = [(a_ref, b * SUB) for b in range(blocks)] + [(z_ref, 0)]
    for slot in range(slots):

        def other(row, chunk, slot=slot):
            return spread(z_ref, row, 0, chunk, slot), spread(z_ref, row, 1, chunk, slot)

        products(x_ref, kept, other, rows, chunks)
        for chunk in range(chunks):
            summed = across(x_ref, rows * len(kept) * 2 * SUB, band_ref, chunk)
            for row in range(rows):
                for place, (_, first) in enumerate(kept):
                    for c in range(2):
                        value = summed[((row * len(kept) + place) * 2 + c) * SUB :][:SUB]
                        if place < blocks:
                            m_ref[slot, row, chunk, c, pl.ds(first, SUB), :] = value
                        else:
                            zz_ref[slot, row, chunk, c] = value

    place = lax.broadcasted_iota(jnp.int32, (SUB, LANES), 0)

    def one_row(chunk, row, carry):
        base = pl.multiple_of((row * chunks + chunk) * 2 * half, SUB)
        scale = r_ref[row, chunk]
        scale_z = rz_ref[row, chunk]
        v_ref[0] = scale
        v_ref[1] = jnp.zeros_like(scale)
        vz_ref[0] = scale_z
        vz_ref[1] = jnp.zeros_like(scale_z)
        for repeat in range(ITERS):
            if repeat == 0:
                real, imag = w_ref[row, chunk, 0], w_ref[row, chunk, 1]
            else:
                real, imag = matvec(s_ref, v_ref, base, dates)
                real, imag = real * (scale / AREA), imag * (scale / AREA)
            add_real, add_imag = jnp.zeros_like(real), jnp.zeros_like(imag)
            z_real, z_imag = jnp.zeros_like(scale_z), jnp.zeros_like(scale_z)
            old_real, old_imag = v_ref[0], v_ref[1]
            for slot in range(slots):
                v_real, v_imag = vz_ref[0, pl.ds(slot, 1), :], vz_ref[1, pl.ds(slot, 1), :]
                m_real, m_imag = m_ref[slot, row, chunk, 0], m_ref[slot, row, chunk, 1]
                add_real = add_real + m_real * v_real - m_imag * v_imag
                add_imag = add_imag + m_real * v_imag + m_imag * v_real
                sum_real = jnp.sum(m_real * old_real + m_imag * old_imag, axis=0, keepdims=True)
                sum_imag = jnp.sum(m_real * old_imag - m_imag * old_real, axis=0, keepdims=True)
                z_real = z_real + jnp.where(place == slot, sum_real, 0.0)
                z_imag = z_imag + jnp.where(place == slot, sum_imag, 0.0)
                zz_real, zz_imag = zz_ref[slot, row, chunk, 0], zz_ref[slot, row, chunk, 1]
                z_real = z_real + zz_real * v_real - zz_imag * v_imag
                z_imag = z_imag + zz_real * v_imag + zz_imag * v_real
            real = real + add_real * (scale / AREA)
            imag = imag + add_imag * (scale / AREA)
            z_real = jnp.where(place < slots, z_real * (scale_z / AREA), 0.0)
            z_imag = jnp.where(place < slots, z_imag * (scale_z / AREA), 0.0)
            square = total_square(real, imag) + total_square(z_real, z_imag)
            factor = lax.rsqrt(square / (slots + dates) + EPSILON)
            real, imag = real * factor, imag * factor
            if repeat < ITERS - 1:
                v_ref[0] = real * scale
                v_ref[1] = imag * scale
                vz_ref[0] = z_real * factor * scale_z
                vz_ref[1] = z_imag * factor * scale_z
        out_ref[row, chunk, 0] = real
        out_ref[row, chunk, 1] = imag
        return carry

    each_row(rows, chunks, one_row)


def vmem():
    return pl.BlockSpec(memory_space=pltpu.VMEM)


def params(limit=24):
    return pltpu.CompilerParams(vmem_limit_bytes=limit * 2**20)


def link_own(a, band, group=4):
    rows, chunks, dates = a.shape[0] - 2 * HALF, a.shape[2], a.shape[3]
    return pl.pallas_call(
        own_kernel,
        out_shape=(
            jax.ShapeDtypeStruct((rows * chunks * 2 * dates * dates, LANES), F32),
            jax.ShapeDtypeStruct((rows, chunks, dates, LANES), F32),
            jax.ShapeDtypeStruct((rows, chunks, 2, dates, LANES), F32),
            jax.ShapeDtypeStruct((2, chunks, rows, LANES), F32),
        ),
        in_specs=[vmem()] * 2,
        out_specs=[vmem()] * 4,
        scratch_shapes=[pltpu.VMEM((2, dates, LANES), F32)]
        + [pltpu.VMEM((rows * 2 * dates, band.shape[0]), BF16)] * group,
        compiler_params=params(),
        name="link_own",
    )(a, band)


def link_window(a, z, band, s, r, w, slots):
    rows, chunks, dates, _ = r.shape
    return pl.pallas_call(
        functools.partial(window_kernel, slots),
        out_shape=jax.ShapeDtypeStruct((rows, chunks, 2, dates, LANES), F32),
        in_specs=[vmem()] * 6,
        out_specs=vmem(),
        scratch_shapes=[
            pltpu.VMEM((rows * 2 * (dates + SUB), band.shape[0]), BF16),
            pltpu.VMEM((slots, rows, chunks, 2, dates, LANES), F32),
            pltpu.VMEM((slots, rows, chunks, 2, SUB, LANES), F32),
            pltpu.VMEM((rows, chunks, SUB, LANES), F32),
            pltpu.VMEM((2, dates, LANES), F32),
            pltpu.VMEM((2, SUB, LANES), F32),
        ],
        compiler_params=params(),
        name="link_window",
    )(a, z, band, s, r, w)


def swap(value, step):
    count = lax.axis_size("date")
    return lax.ppermute(value, "date", [(i, i ^ step) for i in range(count)])


def pick(cond, on_true, on_false):
    return jnp.where(cond, on_true, on_false)


def paired_windows(x):
    slabs = lax.axis_size("pix")
    me = lax.axis_index("date")
    near = me < 2
    even = (me & 1) == 0
    lead = x.transpose(2, 0, 1, 3)
    rows = lead.shape[0] // 4
    reach = 2 * rows + HALF
    low, high = lead[:reach], lead[-reach:]
    top, bottom = lead[:HALF], lead[-HALF:]
    straight, crossed = [], []
    for core in range(2):
        for k in range(slabs):
            if k + 1 < slabs:
                straight.append((core * slabs + k, core * slabs + k + 1))
                crossed.append(((2 + core) * slabs + k, core * slabs + k + 1))
            if k > 0:
                straight.append(((2 + core) * slabs + k, (2 + core) * slabs + k - 1))
                crossed.append((core * slabs + k, (2 + core) * slabs + k - 1))
    edge_own = lax.ppermute(pick(near, bottom, top), ("date", "pix"), straight)
    edge_far = lax.ppermute(pick(near, top, bottom), ("date", "pix"), crossed)
    far = swap(pick(near, high, low), 2)
    own = jnp.concatenate([pick(near, low, high), far], 2)
    edge = jnp.concatenate([edge_own, edge_far], 2)
    both = pick(near, jnp.concatenate([edge, own], 0), jnp.concatenate([own, edge], 0))
    tall = rows + 2 * HALF
    first, second = both[:tall], both[rows:]
    other = swap(pick(even, second, first), 1)
    return jnp.concatenate([pick(even, first, second), other], 2)


def plain_windows(x):
    count, slabs = lax.axis_size("date"), lax.axis_size("pix")
    me = lax.axis_index("date").astype(jnp.uint32)
    lead = x.transpose(2, 0, 1, 3)
    rows = lead.shape[0] // count
    tall = rows + 2 * HALF
    ups = [(k, k + 1) for k in range(slabs - 1)]
    downs = [(b, a) for a, b in ups]
    above = lax.ppermute(lead[-HALF:], "pix", ups)
    below = lax.ppermute(lead[:HALF], "pix", downs)
    padded = jnp.concatenate([above, lead, below], 0)

    def window(target):
        return lax.dynamic_slice_in_dim(padded, target * rows, tall, 0)

    parts = [window(me)] + [swap(window(me ^ step), step) for step in range(1, count)]
    return jnp.concatenate(parts, 2)


def earlier_windows(compressed, shift_by):
    stacks, count, slabs = lax.axis_size("ms"), lax.axis_size("date"), lax.axis_size("pix")
    rows = compressed.shape[1]
    reach = -(-HALF // rows)
    blocks = count * slabs

    def index(stack, block):
        k, d = divmod(block, count)
        return (stack * count + d) * slabs + k

    lead = compressed.transpose(1, 0, 2)
    parts = []
    for offset in range(-reach, reach + 1):
        low = max(0, -HALF - offset * rows)
        high = min(rows, rows + HALF - offset * rows)
        pairs = []
        for stack in range(stacks - shift_by):
            for block in range(blocks):
                target = block - offset
                if 0 <= target < blocks:
                    pairs.append((index(stack, block), index(stack + shift_by, target)))
        parts.append(lax.ppermute(lead[low:high], ("ms", "date", "pix"), pairs))
    return jnp.concatenate(parts, 0)


def assemble_kernel(offsets, place_ref, *refs):
    pieces, (out_ref, mine_ref, whole_ref, sem) = refs[: len(offsets)], refs[len(offsets) :]
    own, rows = out_ref.shape[1], pieces[0].shape[2]
    copies = []
    for offset, piece in zip(offsets, pieces):
        row = pl.multiple_of((place_ref[0] ^ offset) * rows, rows)
        copy = pltpu.make_async_copy(
            piece.at[:, pl.ds(0, own)], out_ref.at[:, :, pl.ds(row, rows), :], sem.at[len(copies)]
        )
        copy.start()
        copies.append(copy)
        whole_ref[:, pl.ds(row, rows), :] = piece[:, own]
    width = mine_ref.shape[3]
    cols = whole_ref.shape[2]
    for c in range(2):
        rolled = pltpu.roll(whole_ref[c], lax.rem(cols - place_ref[0] * width, cols), 1)
        mine_ref[c, 0] = rolled[:, :width]
    for copy in copies:
        copy.wait()


def assemble(pieces, offsets, place, count):
    _, own, rows, cols = pieces[0].shape
    own = own - 1
    return pl.pallas_call(
        functools.partial(assemble_kernel, offsets),
        out_shape=(
            jax.ShapeDtypeStruct((2, own, rows * count, cols), F32),
            jax.ShapeDtypeStruct((2, 1, rows * count, cols // count), F32),
        ),
        in_specs=[pl.BlockSpec(memory_space=pltpu.SMEM)] + [vmem()] * len(pieces),
        out_specs=(pl.BlockSpec(memory_space=pl.ANY), vmem()),
        scratch_shapes=[pltpu.VMEM((2, rows * count, cols), F32), pltpu.SemaphoreType.DMA((len(pieces),))],
        compiler_params=params(8),
        name="assemble",
    )(place, *pieces)


def scatter(blocks, compressed, me, place):
    count = lax.axis_size("date")
    _, own, rows, cols = blocks[0].shape
    if count == 4 and rows % SUB == 0:
        image = compressed[:, None]
        mine, far, sibling, far_sibling = blocks
        got = swap(jnp.concatenate([far, far_sibling, image], 1), 2)
        to_send = jnp.stack(
            [jnp.concatenate([sibling, image], 1), got[:, own:]], 0
        )
        near = swap(to_send, 1)
        pieces = [
            jnp.concatenate([mine, image], 1),
            jnp.concatenate([got[:, :own], got[:, 2 * own :]], 1),
            near[0],
            near[1],
        ]
        return assemble(pieces, (0, 2, 1, 3), place, count)
    out = jnp.zeros((2, own + 1, rows * count, cols), F32)
    for step in range(count):
        piece = jnp.concatenate([blocks[step], compressed[:, None]], 1)
        piece = swap(piece, step) if step else piece
        out = lax.dynamic_update_slice_in_dim(out, piece, (me ^ step) * rows, 2)
    width = cols // count
    return (out[:, :own], lax.dynamic_slice_in_dim(out[:, own:], me * width, width, 3))


def body(slc_stack):
    count = lax.axis_size("date")
    rows = slc_stack.shape[2] // count
    a = paired_windows(slc_stack) if count == 4 and rows >= HALF else plain_windows(slc_stack)
    cols = a.shape[3]
    chunks = cols // LANES
    a = a.reshape(a.shape[:3] + (chunks, LANES)).transpose(0, 1, 3, 2, 4)
    places = jnp.arange(cols, dtype=jnp.int32)
    band = (jnp.abs(places[:, None] - places[None, :]) <= HALF).astype(BF16)
    band = jnp.concatenate([band, band], 0)
    me = lax.axis_index("date").astype(jnp.uint32)
    place = lax.axis_index("date").astype(jnp.int32).reshape(1)
    a, me, place = lax.optimization_barrier((a, me, place))
    s, r, w, compressed = link_own(a, band)
    compressed = compressed.transpose(0, 2, 1, 3).reshape(2, rows, cols)
    slots = min(3, lax.axis_size("ms") - 1)
    z = jnp.stack([earlier_windows(compressed, shift_by) for shift_by in range(1, slots + 1)], 2)
    z = jnp.pad(z, ((0, 0), (0, 0), (0, SUB - slots), (0, 0)))
    z = z.reshape(z.shape[:3] + (chunks, LANES)).transpose(0, 1, 3, 2, 4)
    linked = link_window(a, z, band, s, r, w, slots)
    own = slc_stack.shape[1]
    blocks = [
        linked[:, :, :, j * own : (j + 1) * own].transpose(2, 3, 0, 1, 4).reshape(2, own, rows, cols)
        for j in range(count)
    ]
    return scatter(blocks, compressed, me, place)


def solution(mesh):
    in_specs = (P(None, ("ms", "date"), "pix", None),)
    out_specs = (P(None, ("ms", "date"), "pix", None), P(None, "ms", "pix", "date"))
    return jax.shard_map(body, mesh=mesh, in_specs=in_specs, out_specs=out_specs, check_vma=False)
```

```python
import functools
import math

import jax
import jax.numpy as jnp
from jax import lax
from jax.experimental import pallas as pl
from jax.experimental.pallas import tpu as pltpu
from jax.sharding import PartitionSpec as P

HALF = 5
ITERS = 3
WIDTH = 2 * HALF + 1
AREA = float(WIDTH**2)
EPSILON = 1e-06
SUB = 8
LANES = 128
F32 = jnp.float32
BF16 = jnp.bfloat16


def row_sums(values, count):
    suffix = [None] * WIDTH
    running = values[WIDTH - 1]
    suffix[WIDTH - 1] = running
    for row in range(WIDTH - 2, -1, -1):
        running = running + values[row]
        suffix[row] = running
    out = [suffix[0]]
    prefix = None
    for row in range(1, count):
        term = values[WIDTH - 1 + row]
        prefix = term if prefix is None else prefix + term
        out.append(suffix[row] + prefix)
    return out


def put_split(x_ref, at, chunk, value):
    high = value.astype(BF16)
    low = (value - high.astype(F32)).astype(BF16)
    total = x_ref.shape[1] // 2
    x_ref[pl.ds(at, value.shape[0]), pl.ds(chunk * LANES, LANES)] = high
    x_ref[pl.ds(at, value.shape[0]), pl.ds(total + chunk * LANES, LANES)] = low


def products(x_ref, blocks, other, rows, chunks):
    for chunk in range(chunks):
        for place, (ref, first) in enumerate(blocks):
            at = pl.ds(first, SUB)
            real, imag = [], []
            for row in range(rows + 2 * HALF):
                left_real, left_imag = ref[row, 0, chunk, at, :], ref[row, 1, chunk, at, :]
                right_real, right_imag = other(row, chunk)
                real.append(left_real * right_real + left_imag * right_imag)
                imag.append(left_imag * right_real - left_real * right_imag)
            sums = zip(row_sums(real, rows), row_sums(imag, rows))
            for row, both in enumerate(sums):
                put_split(x_ref, (row * len(blocks) + place) * 2 * SUB, chunk, jnp.concatenate(both, 0))


def energies(x_ref, ref, rows, chunks, dates):
    step = math.gcd(dates, 2 * SUB)
    for chunk in range(chunks):
        for first in range(0, dates, step):
            at = pl.ds(first, step)
            values = []
            for row in range(rows + 2 * HALF):
                real, imag = ref[row, 0, chunk, at, :], ref[row, 1, chunk, at, :]
                values.append(real * real + imag * imag)
            for row, total in enumerate(row_sums(values, rows)):
                put_split(x_ref, row * dates + first, chunk, total)


def across(x_ref, size, band_ref, chunk):
    band = band_ref[:, pl.ds(chunk * LANES, LANES)]
    return jnp.dot(x_ref[0:size, :], band, preferred_element_type=F32)


def spread(ref, *place):
    return ref[place[:-1] + (pl.ds(place[-1], SUB, stride=0), slice(None))]


def pitch(dates):
    return dates if (dates // SUB) % 2 else dates + SUB


def accumulate(total, term):
    return term if total is None else total + term


def matvec(s_ref, v_ref, base, dates):
    blocks = dates // SUB
    real, imag = [None] * blocks, [None] * blocks
    for q in range(dates):
        v_real, v_imag = spread(v_ref, 0, q), spread(v_ref, 1, q)
        for b in range(blocks):
            at = q * pitch(dates) + b * SUB
            s_real = s_ref[pl.ds(base + at, SUB), :]
            s_imag = s_ref[pl.ds(base + dates * pitch(dates) + at, SUB), :]
            real[b] = accumulate(real[b], s_real * v_real - s_imag * v_imag)
            imag[b] = accumulate(imag[b], s_real * v_imag + s_imag * v_real)
    return jnp.concatenate(real, 0), jnp.concatenate(imag, 0)


def fill_and_apply(s_ref, v_ref, base, dates):
    blocks = dates // SUB
    real, imag = [None] * blocks, [None] * blocks
    half = dates * pitch(dates)
    for q in range(dates):
        v_real = spread(v_ref, 0, q)
        for b in range(blocks):
            at = pl.ds(base + q * pitch(dates) + b * SUB, SUB)
            at_imag = pl.ds(base + half + q * pitch(dates) + b * SUB, SUB)
            if b < q // SUB:
                turned = base + b * SUB * pitch(dates) + q
                s_real = s_ref[pl.ds(turned, SUB, stride=pitch(dates)), :]
                s_imag = -s_ref[pl.ds(turned + half, SUB, stride=pitch(dates)), :]
                s_ref[at, :] = s_real
                s_ref[at_imag, :] = s_imag
            else:
                s_real, s_imag = s_ref[at, :], s_ref[at_imag, :]
            real[b] = accumulate(real[b], s_real * v_real)
            imag[b] = accumulate(imag[b], s_imag * v_real)
    return jnp.concatenate(real, 0), jnp.concatenate(imag, 0)


def total_square(real, imag):
    return jnp.sum(real * real + imag * imag, axis=0, keepdims=True)


def each_row(rows, chunks, one_row):
    for chunk in range(chunks):
        lax.fori_loop(0, rows, functools.partial(one_row, chunk), 0)


def own_kernel(a_ref, band_ref, s_ref, r_ref, w_ref, comp_ref, v_ref, *x_refs):
    rows, chunks, dates, _ = r_ref.shape
    blocks = dates // SUB
    half = dates * pitch(dates)
    group = len(x_refs)

    energies(x_refs[0], a_ref, rows, chunks, dates)
    for chunk in range(chunks):
        power = across(x_refs[0], rows * dates, band_ref, chunk)
        scale = lax.rsqrt(power / AREA + EPSILON)
        r_ref[:, chunk] = scale.reshape(rows, dates, LANES)

    for q_block in range(blocks):
        kept = [(a_ref, b * SUB) for b in range(q_block, blocks)]

        def one_group(turn, carry, q_block=q_block, kept=kept):
            for u in range(group):
                q = q_block * SUB + turn * group + u

                def other(row, chunk, q=q):
                    return spread(a_ref, row, 0, chunk, q), spread(a_ref, row, 1, chunk, q)

                products(x_refs[u], kept, other, rows, chunks)
                for chunk in range(chunks):
                    summed = across(x_refs[u], rows * len(kept) * 2 * SUB, band_ref, chunk)
                    for row in range(rows):
                        for place, (_, first) in enumerate(kept):
                            for c in range(2):
                                value = summed[((row * len(kept) + place) * 2 + c) * SUB :][:SUB]
                                at = (row * chunks + chunk) * 2 * half + c * half + q * pitch(dates) + first
                                s_ref[pl.ds(pl.multiple_of(at, SUB), SUB), :] = value
            return carry

        lax.fori_loop(0, SUB // group, one_group, 0)

    def one_row(chunk, row, carry):
        base = pl.multiple_of((row * chunks + chunk) * 2 * half, SUB)
        scale = r_ref[row, chunk]
        v_ref[0] = scale
        for repeat in range(ITERS):
            if repeat == 0:
                real, imag = fill_and_apply(s_ref, v_ref, base, dates)
            else:
                real, imag = matvec(s_ref, v_ref, base, dates)
            real, imag = real * (scale / AREA), imag * (scale / AREA)
            if repeat == 0:
                w_ref[row, chunk, 0] = real
                w_ref[row, chunk, 1] = imag
            factor = lax.rsqrt(total_square(real, imag) / dates + EPSILON)
            real, imag = real * factor, imag * factor
            if repeat < ITERS - 1:
                v_ref[0] = real * scale
                v_ref[1] = imag * scale
        centre_real, centre_imag = a_ref[row + HALF, 0, chunk], a_ref[row + HALF, 1, chunk]
        root = math.sqrt(dates)
        comp_real = jnp.sum(real * centre_real + imag * centre_imag, axis=0, keepdims=True)
        comp_imag = jnp.sum(real * centre_imag - imag * centre_real, axis=0, keepdims=True)
        comp_ref[0, chunk, pl.ds(row, 1), :] = comp_real / root
        comp_ref[1, chunk, pl.ds(row, 1), :] = comp_imag / root
        return carry

    each_row(rows, chunks, one_row)


def block_of(date, slab):
    return date ^ (2 * (slab & 1))


def fill_window(z_ref, images):
    centre_ref, sibling_ref, other_ref = images
    slab, slabs = lax.axis_index("pix"), lax.axis_size("pix")
    block = block_of(lax.axis_index("date"), slab)
    even = (block & 1) == 0
    known = lax.axis_index("ms") > 0
    inner = known & jnp.logical_not(((slab == 0) & (block == 0)) | ((slab == slabs - 1) & (block == 3)))
    sibling = jnp.where(known, sibling_ref[...], 0.0)
    other = jnp.where(inner, other_ref[...], 0.0)
    z_ref[0] = jnp.where(even, other, sibling)
    z_ref[1] = jnp.where(known, centre_ref[...], 0.0)
    z_ref[2] = jnp.where(even, sibling, other)


class Row:
    def __init__(self, z_ref, rows):
        self.z_ref, self.rows = z_ref, rows

    def __getitem__(self, index):
        row, c, chunk = index[:3]
        part, at = divmod(row - HALF + self.rows, self.rows)
        return spread(self.z_ref, part, c, chunk, at)


def window_kernel(slots, paired, *refs):
    a_ref, band_ref, s_ref, r_ref, w_ref = refs[:5]
    rows, chunks, dates, _ = r_ref.shape
    count = 3 if paired else 1
    images = refs[5 : 5 + count]
    out_ref, x_ref, m_ref, zz_ref, rz_ref, v_ref, vz_ref = refs[5 + count : 12 + count]
    blocks = dates // SUB
    half = dates * pitch(dates)
    if paired:
        fill_window(refs[12 + count], images)
        z = Row(refs[12 + count], rows)
    else:
        z = images[0]
        energies(x_ref, z, rows, chunks, SUB)
        for chunk in range(chunks):
            power = across(x_ref, rows * SUB, band_ref, chunk)
            rz_ref[:, chunk] = lax.rsqrt(power / AREA + EPSILON).reshape(rows, SUB, LANES)

    kept = [(a_ref, b * SUB) for b in range(blocks)] + [(z, 0)]
    for slot in range(slots):

        def other(row, chunk, slot=slot):
            if paired:
                return z[row, 0, chunk], z[row, 1, chunk]
            return spread(z, row, 0, chunk, slot), spread(z, row, 1, chunk, slot)

        products(x_ref, kept, other, rows, chunks)
        for chunk in range(chunks):
            summed = across(x_ref, rows * len(kept) * 2 * SUB, band_ref, chunk)
            for row in range(rows):
                for place, (_, first) in enumerate(kept):
                    for c in range(2):
                        value = summed[((row * len(kept) + place) * 2 + c) * SUB :][:SUB]
                        if place < blocks:
                            m_ref[slot, row, chunk, c, pl.ds(first, SUB), :] = value
                        else:
                            zz_ref[slot, row, chunk, c] = value
                            if paired and c == 0:
                                rz_ref[row, chunk] = lax.rsqrt(value / AREA + EPSILON)

    place = lax.broadcasted_iota(jnp.int32, (SUB, LANES), 0)

    def one_row(chunk, row, carry):
        base = pl.multiple_of((row * chunks + chunk) * 2 * half, SUB)
        scale = r_ref[row, chunk]
        scale_z = rz_ref[row, chunk]
        v_ref[0] = scale
        v_ref[1] = jnp.zeros_like(scale)
        vz_ref[0] = scale_z
        vz_ref[1] = jnp.zeros_like(scale_z)
        for repeat in range(ITERS):
            if repeat == 0:
                real, imag = w_ref[row, chunk, 0], w_ref[row, chunk, 1]
            else:
                real, imag = matvec(s_ref, v_ref, base, dates)
                real, imag = real * (scale / AREA), imag * (scale / AREA)
            add_real, add_imag = jnp.zeros_like(real), jnp.zeros_like(imag)
            z_real, z_imag = jnp.zeros_like(scale_z), jnp.zeros_like(scale_z)
            old_real, old_imag = v_ref[0], v_ref[1]
            for slot in range(slots):
                v_real, v_imag = vz_ref[0, pl.ds(slot, 1), :], vz_ref[1, pl.ds(slot, 1), :]
                m_real, m_imag = m_ref[slot, row, chunk, 0], m_ref[slot, row, chunk, 1]
                add_real = add_real + m_real * v_real - m_imag * v_imag
                add_imag = add_imag + m_real * v_imag + m_imag * v_real
                sum_real = jnp.sum(m_real * old_real + m_imag * old_imag, axis=0, keepdims=True)
                sum_imag = jnp.sum(m_real * old_imag - m_imag * old_real, axis=0, keepdims=True)
                z_real = z_real + jnp.where(place == slot, sum_real, 0.0)
                z_imag = z_imag + jnp.where(place == slot, sum_imag, 0.0)
                zz_real, zz_imag = zz_ref[slot, row, chunk, 0], zz_ref[slot, row, chunk, 1]
                z_real = z_real + zz_real * v_real - zz_imag * v_imag
                z_imag = z_imag + zz_real * v_imag + zz_imag * v_real
            real = real + add_real * (scale / AREA)
            imag = imag + add_imag * (scale / AREA)
            z_real = jnp.where(place < slots, z_real * (scale_z / AREA), 0.0)
            z_imag = jnp.where(place < slots, z_imag * (scale_z / AREA), 0.0)
            square = total_square(real, imag) + total_square(z_real, z_imag)
            factor = lax.rsqrt(square / (slots + dates) + EPSILON)
            real, imag = real * factor, imag * factor
            if repeat < ITERS - 1:
                v_ref[0] = real * scale
                v_ref[1] = imag * scale
                vz_ref[0] = z_real * factor * scale_z
                vz_ref[1] = z_imag * factor * scale_z
        out_ref[row, chunk, 0] = real
        out_ref[row, chunk, 1] = imag
        return carry

    each_row(rows, chunks, one_row)


def vmem():
    return pl.BlockSpec(memory_space=pltpu.VMEM)


def params(limit=24):
    return pltpu.CompilerParams(vmem_limit_bytes=limit * 2**20)


def link_own(a, band, group=8):
    rows, chunks, dates = a.shape[0] - 2 * HALF, a.shape[2], a.shape[3]
    return pl.pallas_call(
        own_kernel,
        out_shape=(
            jax.ShapeDtypeStruct((rows * chunks * 2 * dates * pitch(dates), LANES), F32),
            jax.ShapeDtypeStruct((rows, chunks, dates, LANES), F32),
            jax.ShapeDtypeStruct((rows, chunks, 2, dates, LANES), F32),
            jax.ShapeDtypeStruct((2, chunks, rows, LANES), F32),
        ),
        in_specs=[vmem()] * 2,
        out_specs=[vmem()] * 4,
        scratch_shapes=[pltpu.VMEM((2, dates, LANES), F32)]
        + [pltpu.VMEM((rows * 2 * dates, band.shape[0]), BF16)] * group,
        compiler_params=params(),
        name="link_own",
    )(a, band)


def link_window(a, images, band, s, r, w, slots, paired):
    rows, chunks, dates, _ = r.shape
    scratch = [
        pltpu.VMEM((rows * 2 * (dates + SUB), band.shape[0]), BF16),
        pltpu.VMEM((slots, rows, chunks, 2, dates, LANES), F32),
        pltpu.VMEM((slots, rows, chunks, 2, SUB, LANES), F32),
        pltpu.VMEM((rows, chunks, SUB, LANES), F32),
        pltpu.VMEM((2, dates, LANES), F32),
        pltpu.VMEM((2, SUB, LANES), F32),
    ]
    if paired:
        scratch.append(pltpu.VMEM((3, 2, chunks, rows, LANES), F32))
    return pl.pallas_call(
        functools.partial(window_kernel, slots, paired),
        out_shape=jax.ShapeDtypeStruct((rows, chunks, 2, dates, LANES), F32),
        in_specs=[vmem()] * (5 + len(images)),
        out_specs=vmem(),
        scratch_shapes=scratch,
        compiler_params=params(),
        name="link_window",
    )(a, band, s, r, w, *images)


def swap(value, step):
    count = lax.axis_size("date")
    return lax.ppermute(value, "date", [(i, i ^ step) for i in range(count)])


def pick(cond, on_true, on_false):
    return jnp.where(cond, on_true, on_false)


def is_paired(x):
    return lax.axis_size("ms") == 2 and lax.axis_size("date") == 4 and x.shape[2] % (4 * SUB) == 0


def paired_windows(x):
    slabs = lax.axis_size("pix")
    block = block_of(lax.axis_index("date"), lax.axis_index("pix"))
    near = block < 2
    even = (block & 1) == 0
    lead = x.transpose(2, 0, 1, 3)
    rows = lead.shape[0] // 4
    reach = 2 * rows + HALF
    low, high = lead[:reach], lead[-reach:]
    pairs = []
    for date in range(4):
        for k in range(slabs):
            target = k - 1 if block_of(date, k) < 2 else k + 1
            if 0 <= target < slabs:
                pairs.append((date * slabs + k, date * slabs + target))
            else:
                pairs.append((date * slabs + k, (date ^ 1) * slabs + k))
    outer = pick(near, lax.axis_index("pix") == 0, lax.axis_index("pix") == slabs - 1)

    def edge_rows(rows_of):
        got = lax.ppermute(pick(near, rows_of[:HALF], rows_of[-HALF:]), ("date", "pix"), pairs)
        return pick(outer, jnp.zeros_like(got), got)

    here = pick(near, low, high)
    far = swap(pick(near, high, low), 2)
    edge = jnp.concatenate([edge_rows(here), edge_rows(far)], 2)
    own = jnp.concatenate([here, far], 2)
    both = pick(near, jnp.concatenate([edge, own], 0), jnp.concatenate([own, edge], 0))
    tall = rows + 2 * HALF
    first, second = both[:tall], both[rows:]
    other = swap(pick(even, second, first), 1)
    return jnp.concatenate([pick(even, first, second), other], 2)


def plain_windows(x):
    count, slabs = lax.axis_size("date"), lax.axis_size("pix")
    me = lax.axis_index("date").astype(jnp.uint32)
    lead = x.transpose(2, 0, 1, 3)
    rows = lead.shape[0] // count
    tall = rows + 2 * HALF
    ups = [(k, k + 1) for k in range(slabs - 1)]
    downs = [(b, a) for a, b in ups]
    above = lax.ppermute(lead[-HALF:], "pix", ups)
    below = lax.ppermute(lead[:HALF], "pix", downs)
    padded = jnp.concatenate([above, lead, below], 0)

    def window(target):
        return lax.dynamic_slice_in_dim(padded, target * rows, tall, 0)

    parts = [window(me)] + [swap(window(me ^ step), step) for step in range(1, count)]
    return jnp.concatenate(parts, 2)


def earlier_windows(compressed, shift_by):
    stacks, count, slabs = lax.axis_size("ms"), lax.axis_size("date"), lax.axis_size("pix")
    rows = compressed.shape[1]
    reach = -(-HALF // rows)
    blocks = count * slabs

    def index(stack, block):
        k, d = divmod(block, count)
        return (stack * count + d) * slabs + k

    lead = compressed.transpose(1, 0, 2)
    parts = []
    for offset in range(-reach, reach + 1):
        low = max(0, -HALF - offset * rows)
        high = min(rows, rows + HALF - offset * rows)
        pairs = []
        for stack in range(stacks - shift_by):
            for block in range(blocks):
                target = block - offset
                if 0 <= target < blocks:
                    pairs.append((index(stack, block), index(stack + shift_by, target)))
        parts.append(lax.ppermute(lead[low:high], ("ms", "date", "pix"), pairs))
    return jnp.concatenate(parts, 0)


def assemble_kernel(offsets, *refs):
    date = lax.axis_index("date")
    block = block_of(date, lax.axis_index("pix"))
    pieces, (out_ref, mine_ref, whole_ref, sem) = refs[: len(offsets)], refs[len(offsets) :]
    own, rows = out_ref.shape[1], pieces[0].shape[2]
    copies = []
    for offset, piece in zip(offsets, pieces):
        row = pl.multiple_of((block ^ offset) * rows, rows)
        copy = pltpu.make_async_copy(
            piece.at[:, pl.ds(0, own)], out_ref.at[:, :, pl.ds(row, rows), :], sem.at[len(copies)]
        )
        copy.start()
        copies.append(copy)
        whole_ref[:, pl.ds(row, rows), :] = piece[:, own]
    width = mine_ref.shape[3]
    cols = whole_ref.shape[2]
    for c in range(2):
        rolled = pltpu.roll(whole_ref[c], lax.rem(cols - date * width, cols), 1)
        mine_ref[c, 0] = rolled[:, :width]
    for copy in copies:
        copy.wait()


def assemble(pieces, offsets, count):
    _, own, rows, cols = pieces[0].shape
    own = own - 1
    return pl.pallas_call(
        functools.partial(assemble_kernel, offsets),
        out_shape=(
            jax.ShapeDtypeStruct((2, own, rows * count, cols), F32),
            jax.ShapeDtypeStruct((2, 1, rows * count, cols // count), F32),
        ),
        in_specs=[vmem()] * len(pieces),
        out_specs=(pl.BlockSpec(memory_space=pl.ANY), vmem()),
        scratch_shapes=[pltpu.VMEM((2, rows * count, cols), F32), pltpu.SemaphoreType.DMA((len(pieces),))],
        compiler_params=params(8),
        name="assemble",
    )(*pieces)


def scatter(blocks, compressed, me, paired):
    count = lax.axis_size("date")
    _, own, rows, cols = blocks[0].shape
    if paired:
        image = compressed[:, None]
        mine, far, sibling, far_sibling = blocks
        got = swap(jnp.concatenate([far, far_sibling, image], 1), 2)
        to_send = jnp.stack(
            [jnp.concatenate([sibling, image], 1), got[:, own:]], 0
        )
        near = swap(to_send, 1)
        pieces = [
            jnp.concatenate([mine, image], 1),
            jnp.concatenate([got[:, :own], got[:, 2 * own :]], 1),
            near[0],
            near[1],
        ]
        return assemble(pieces, (0, 2, 1, 3), count)
    out = jnp.zeros((2, own + 1, rows * count, cols), F32)
    for step in range(count):
        piece = jnp.concatenate([blocks[step], compressed[:, None]], 1)
        piece = swap(piece, step) if step else piece
        out = lax.dynamic_update_slice_in_dim(out, piece, (me ^ step) * rows, 2)
    width = cols // count
    return (out[:, :own], lax.dynamic_slice_in_dim(out[:, own:], me * width, width, 3))


def earlier_images(compressed):
    slabs = lax.axis_size("pix")
    blocks = 4 * slabs

    def index(stack, block):
        k, t = divmod(block, 4)
        return (stack * 4 + block_of(t, k)) * slabs + k

    def crossing(block):
        target = block + 1 if block & 1 else block - 1
        return target if 0 <= target < blocks else block

    def move(target_of):
        pairs = [
            (index(stack, block), index(1 - stack, target_of(block))) for stack in range(2) for block in range(blocks)
        ]
        return lax.ppermute(compressed, ("ms", "date", "pix"), pairs)

    return [move(lambda block: block), move(lambda block: block ^ 1), move(crossing)]


def body(slc_stack):
    count = lax.axis_size("date")
    rows = slc_stack.shape[2] // count
    paired = is_paired(slc_stack)
    a = paired_windows(slc_stack) if paired else plain_windows(slc_stack)
    cols = a.shape[3]
    chunks = cols // LANES
    a = a.reshape(a.shape[:3] + (chunks, LANES)).transpose(0, 1, 3, 2, 4)
    places = jnp.arange(cols, dtype=jnp.int32)
    band = (jnp.abs(places[:, None] - places[None, :]) <= HALF).astype(BF16)
    band = jnp.concatenate([band, band], 0)
    me = lax.axis_index("date").astype(jnp.uint32)
    a, me = lax.optimization_barrier((a, me))
    s, r, w, compressed = link_own(a, band)
    slots = min(3, lax.axis_size("ms") - 1)
    image = compressed.transpose(0, 2, 1, 3).reshape(2, rows, cols)
    if paired:
        images = earlier_images(compressed)
    else:
        z = jnp.stack([earlier_windows(image, shift_by) for shift_by in range(1, slots + 1)], 2)
        z = jnp.pad(z, ((0, 0), (0, 0), (0, SUB - slots), (0, 0)))
        images = [z.reshape(z.shape[:3] + (chunks, LANES)).transpose(0, 1, 3, 2, 4)]
    linked = link_window(a, images, band, s, r, w, slots, paired)
    own = slc_stack.shape[1]
    blocks = [
        linked[:, :, :, j * own : (j + 1) * own].transpose(2, 3, 0, 1, 4).reshape(2, own, rows, cols)
        for j in range(count)
    ]
    return scatter(blocks, image, me, paired)


def solution(mesh):
    in_specs = (P(None, ("ms", "date"), "pix", None),)
    out_specs = (P(None, ("ms", "date"), "pix", None), P(None, "ms", "pix", "date"))
    return jax.shard_map(body, mesh=mesh, in_specs=in_specs, out_specs=out_specs, check_vma=False)
```

```python
import functools
import math

import jax
import jax.numpy as jnp
from jax import lax
from jax.experimental import pallas as pl
from jax.experimental.pallas import tpu as pltpu
from jax.sharding import PartitionSpec as P

HALF = 5
ITERS = 3
WIDTH = 2 * HALF + 1
AREA = float(WIDTH**2)
EPSILON = 1e-06
SUB = 8
LANES = 128
F32 = jnp.float32
BF16 = jnp.bfloat16


def row_sums(values, count):
    suffix = [None] * WIDTH
    running = values[WIDTH - 1]
    suffix[WIDTH - 1] = running
    for row in range(WIDTH - 2, -1, -1):
        running = running + values[row]
        suffix[row] = running
    out = [suffix[0]]
    prefix = None
    for row in range(1, count):
        term = values[WIDTH - 1 + row]
        prefix = term if prefix is None else prefix + term
        out.append(suffix[row] + prefix)
    return out


def put_split(x_ref, at, chunk, value):
    high = value.astype(BF16)
    low = (value - high.astype(F32)).astype(BF16)
    total = x_ref.shape[1] // 2
    x_ref[pl.ds(at, value.shape[0]), pl.ds(chunk * LANES, LANES)] = high
    x_ref[pl.ds(at, value.shape[0]), pl.ds(total + chunk * LANES, LANES)] = low


def products(x_ref, blocks, other, rows, chunks):
    for chunk in range(chunks):
        for place, (ref, first) in enumerate(blocks):
            at = pl.ds(first, SUB)
            real, imag = [], []
            for row in range(rows + 2 * HALF):
                left_real, left_imag = ref[row, 0, chunk, at, :], ref[row, 1, chunk, at, :]
                right_real, right_imag = other(row, chunk)
                real.append(left_real * right_real + left_imag * right_imag)
                imag.append(left_imag * right_real - left_real * right_imag)
            sums = zip(row_sums(real, rows), row_sums(imag, rows))
            for row, both in enumerate(sums):
                put_split(x_ref, (row * len(blocks) + place) * 2 * SUB, chunk, jnp.concatenate(both, 0))


def energies(x_ref, ref, rows, chunks, dates):
    step = math.gcd(dates, 2 * SUB)
    for chunk in range(chunks):
        for first in range(0, dates, step):
            at = pl.ds(first, step)
            values = []
            for row in range(rows + 2 * HALF):
                real, imag = ref[row, 0, chunk, at, :], ref[row, 1, chunk, at, :]
                values.append(real * real + imag * imag)
            for row, total in enumerate(row_sums(values, rows)):
                put_split(x_ref, row * dates + first, chunk, total)


def across(x_ref, size, band_ref, chunk):
    band = band_ref[:, pl.ds(chunk * LANES, LANES)]
    return jnp.dot(x_ref[0:size, :], band, preferred_element_type=F32)


def spread(ref, *place):
    return ref[place[:-1] + (pl.ds(place[-1], SUB, stride=0), slice(None))]


def pitch(dates):
    return dates if (dates // SUB) % 2 else dates + SUB


def accumulate(total, term):
    return term if total is None else total + term


def matvec(s_ref, v_ref, base, dates):
    blocks = dates // SUB
    real, imag = [None] * blocks, [None] * blocks
    for q in range(dates):
        v_real, v_imag = spread(v_ref, 0, q), spread(v_ref, 1, q)
        for b in range(blocks):
            at = q * pitch(dates) + b * SUB
            s_real = s_ref[pl.ds(base + at, SUB), :]
            s_imag = s_ref[pl.ds(base + dates * pitch(dates) + at, SUB), :]
            real[b] = accumulate(real[b], s_real * v_real - s_imag * v_imag)
            imag[b] = accumulate(imag[b], s_real * v_imag + s_imag * v_real)
    return jnp.concatenate(real, 0), jnp.concatenate(imag, 0)


def fill_and_apply(s_ref, v_ref, base, dates):
    blocks = dates // SUB
    real, imag = [None] * blocks, [None] * blocks
    half = dates * pitch(dates)
    for q in range(dates):
        v_real = spread(v_ref, 0, q)
        for b in range(blocks):
            at = pl.ds(base + q * pitch(dates) + b * SUB, SUB)
            at_imag = pl.ds(base + half + q * pitch(dates) + b * SUB, SUB)
            if b < q // SUB:
                turned = base + b * SUB * pitch(dates) + q
                s_real = s_ref[pl.ds(turned, SUB, stride=pitch(dates)), :]
                s_imag = -s_ref[pl.ds(turned + half, SUB, stride=pitch(dates)), :]
                s_ref[at, :] = s_real
                s_ref[at_imag, :] = s_imag
            else:
                s_real, s_imag = s_ref[at, :], s_ref[at_imag, :]
            real[b] = accumulate(real[b], s_real * v_real)
            imag[b] = accumulate(imag[b], s_imag * v_real)
    return jnp.concatenate(real, 0), jnp.concatenate(imag, 0)


def total_square(real, imag):
    return jnp.sum(real * real + imag * imag, axis=0, keepdims=True)


def each_row(rows, chunks, one_row):
    for chunk in range(chunks):
        lax.fori_loop(0, rows, functools.partial(one_row, chunk), 0)


def own_kernel(a_ref, band_ref, s_ref, r_ref, w_ref, comp_ref, v_ref, *x_refs):
    rows, chunks, dates, _ = r_ref.shape
    blocks = dates // SUB
    half = dates * pitch(dates)
    group = len(x_refs)

    energies(x_refs[0], a_ref, rows, chunks, dates)
    for chunk in range(chunks):
        power = across(x_refs[0], rows * dates, band_ref, chunk)
        scale = lax.rsqrt(power / AREA + EPSILON)
        r_ref[:, chunk] = scale.reshape(rows, dates, LANES)

    for q_block in range(blocks):
        kept = [(a_ref, b * SUB) for b in range(q_block, blocks)]

        def one_group(turn, carry, q_block=q_block, kept=kept):
            for u in range(group):
                q = q_block * SUB + turn * group + u

                def other(row, chunk, q=q):
                    return spread(a_ref, row, 0, chunk, q), spread(a_ref, row, 1, chunk, q)

                products(x_refs[u], kept, other, rows, chunks)
                for chunk in range(chunks):
                    summed = across(x_refs[u], rows * len(kept) * 2 * SUB, band_ref, chunk)
                    for row in range(rows):
                        for place, (_, first) in enumerate(kept):
                            for c in range(2):
                                value = summed[((row * len(kept) + place) * 2 + c) * SUB :][:SUB]
                                at = (row * chunks + chunk) * 2 * half + c * half + q * pitch(dates) + first
                                s_ref[pl.ds(pl.multiple_of(at, SUB), SUB), :] = value
            return carry

        lax.fori_loop(0, SUB // group, one_group, 0)

    def one_row(chunk, row, carry):
        base = pl.multiple_of((row * chunks + chunk) * 2 * half, SUB)
        scale = r_ref[row, chunk]
        v_ref[0] = scale
        for repeat in range(ITERS):
            if repeat == 0:
                real, imag = fill_and_apply(s_ref, v_ref, base, dates)
            else:
                real, imag = matvec(s_ref, v_ref, base, dates)
            real, imag = real * (scale / AREA), imag * (scale / AREA)
            if repeat == 0:
                w_ref[row, chunk, 0] = real
                w_ref[row, chunk, 1] = imag
            factor = lax.rsqrt(total_square(real, imag) / dates + EPSILON)
            real, imag = real * factor, imag * factor
            if repeat < ITERS - 1:
                v_ref[0] = real * scale
                v_ref[1] = imag * scale
        centre_real, centre_imag = a_ref[row + HALF, 0, chunk], a_ref[row + HALF, 1, chunk]
        root = math.sqrt(dates)
        comp_real = jnp.sum(real * centre_real + imag * centre_imag, axis=0, keepdims=True)
        comp_imag = jnp.sum(real * centre_imag - imag * centre_real, axis=0, keepdims=True)
        comp_ref[0, chunk, pl.ds(row, 1), :] = comp_real / root
        comp_ref[1, chunk, pl.ds(row, 1), :] = comp_imag / root
        return carry

    each_row(rows, chunks, one_row)


def block_of(date, slab):
    return date ^ (2 * (slab & 1))


def fill_window(z_ref, images):
    centre_ref, sibling_ref, other_ref = images
    slab, slabs = lax.axis_index("pix"), lax.axis_size("pix")
    block = block_of(lax.axis_index("date"), slab)
    even = (block & 1) == 0
    known = lax.axis_index("ms") > 0
    inner = known & jnp.logical_not(((slab == 0) & (block == 0)) | ((slab == slabs - 1) & (block == 3)))
    sibling = jnp.where(known, sibling_ref[...], 0.0)
    other = jnp.where(inner, other_ref[...], 0.0)
    z_ref[0] = jnp.where(even, other, sibling)
    z_ref[1] = jnp.where(known, centre_ref[...], 0.0)
    z_ref[2] = jnp.where(even, sibling, other)


class Row:
    def __init__(self, z_ref, rows):
        self.z_ref, self.rows = z_ref, rows

    def __getitem__(self, index):
        row, c, chunk = index[:3]
        part, at = divmod(row - HALF + self.rows, self.rows)
        return spread(self.z_ref, part, c, chunk, at)


def window_kernel(slots, paired, *refs):
    a_ref, band_ref, s_ref, r_ref, w_ref = refs[:5]
    rows, chunks, dates, _ = r_ref.shape
    count = 3 if paired else 1
    images = refs[5 : 5 + count]
    out_ref, x_ref, m_ref, zz_ref, rz_ref, v_ref, vz_ref = refs[5 + count : 12 + count]
    blocks = dates // SUB
    half = dates * pitch(dates)
    if paired:
        fill_window(refs[12 + count], images)
        z = Row(refs[12 + count], rows)
    else:
        z = images[0]
        energies(x_ref, z, rows, chunks, SUB)
        for chunk in range(chunks):
            power = across(x_ref, rows * SUB, band_ref, chunk)
            rz_ref[:, chunk] = lax.rsqrt(power / AREA + EPSILON).reshape(rows, SUB, LANES)

    kept = [(a_ref, b * SUB) for b in range(blocks)] + [(z, 0)]
    for slot in range(slots):

        def other(row, chunk, slot=slot):
            if paired:
                return z[row, 0, chunk], z[row, 1, chunk]
            return spread(z, row, 0, chunk, slot), spread(z, row, 1, chunk, slot)

        products(x_ref, kept, other, rows, chunks)
        for chunk in range(chunks):
            summed = across(x_ref, rows * len(kept) * 2 * SUB, band_ref, chunk)
            for row in range(rows):
                for place, (_, first) in enumerate(kept):
                    for c in range(2):
                        value = summed[((row * len(kept) + place) * 2 + c) * SUB :][:SUB]
                        if place < blocks:
                            m_ref[slot, row, chunk, c, pl.ds(first, SUB), :] = value
                        else:
                            zz_ref[slot, row, chunk, c] = value
                            if paired and c == 0:
                                rz_ref[row, chunk] = lax.rsqrt(value / AREA + EPSILON)

    place = lax.broadcasted_iota(jnp.int32, (SUB, LANES), 0)

    def one_row(chunk, row, carry):
        base = pl.multiple_of((row * chunks + chunk) * 2 * half, SUB)
        scale = r_ref[row, chunk]
        scale_z = rz_ref[row, chunk]
        v_ref[0] = scale
        v_ref[1] = jnp.zeros_like(scale)
        vz_ref[0] = scale_z
        vz_ref[1] = jnp.zeros_like(scale_z)
        for repeat in range(ITERS):
            if repeat == 0:
                real, imag = w_ref[row, chunk, 0], w_ref[row, chunk, 1]
            else:
                real, imag = matvec(s_ref, v_ref, base, dates)
                real, imag = real * (scale / AREA), imag * (scale / AREA)
            add_real, add_imag = jnp.zeros_like(real), jnp.zeros_like(imag)
            z_real, z_imag = jnp.zeros_like(scale_z), jnp.zeros_like(scale_z)
            old_real, old_imag = v_ref[0], v_ref[1]
            for slot in range(slots):
                v_real, v_imag = vz_ref[0, pl.ds(slot, 1), :], vz_ref[1, pl.ds(slot, 1), :]
                m_real, m_imag = m_ref[slot, row, chunk, 0], m_ref[slot, row, chunk, 1]
                add_real = add_real + m_real * v_real - m_imag * v_imag
                add_imag = add_imag + m_real * v_imag + m_imag * v_real
                sum_real = jnp.sum(m_real * old_real + m_imag * old_imag, axis=0, keepdims=True)
                sum_imag = jnp.sum(m_real * old_imag - m_imag * old_real, axis=0, keepdims=True)
                z_real = z_real + jnp.where(place == slot, sum_real, 0.0)
                z_imag = z_imag + jnp.where(place == slot, sum_imag, 0.0)
                zz_real, zz_imag = zz_ref[slot, row, chunk, 0], zz_ref[slot, row, chunk, 1]
                z_real = z_real + zz_real * v_real - zz_imag * v_imag
                z_imag = z_imag + zz_real * v_imag + zz_imag * v_real
            real = real + add_real * (scale / AREA)
            imag = imag + add_imag * (scale / AREA)
            z_real = jnp.where(place < slots, z_real * (scale_z / AREA), 0.0)
            z_imag = jnp.where(place < slots, z_imag * (scale_z / AREA), 0.0)
            square = total_square(real, imag) + total_square(z_real, z_imag)
            factor = lax.rsqrt(square / (slots + dates) + EPSILON)
            real, imag = real * factor, imag * factor
            if repeat < ITERS - 1:
                v_ref[0] = real * scale
                v_ref[1] = imag * scale
                vz_ref[0] = z_real * factor * scale_z
                vz_ref[1] = z_imag * factor * scale_z
        out_ref[row, chunk, 0] = real
        out_ref[row, chunk, 1] = imag
        return carry

    each_row(rows, chunks, one_row)


def vmem():
    return pl.BlockSpec(memory_space=pltpu.VMEM)


def params(limit=24):
    return pltpu.CompilerParams(vmem_limit_bytes=limit * 2**20)


def link_own(a, band, group=8):
    rows, chunks, dates = a.shape[0] - 2 * HALF, a.shape[2], a.shape[3]
    return pl.pallas_call(
        own_kernel,
        out_shape=(
            jax.ShapeDtypeStruct((rows * chunks * 2 * dates * pitch(dates), LANES), F32),
            jax.ShapeDtypeStruct((rows, chunks, dates, LANES), F32),
            jax.ShapeDtypeStruct((rows, chunks, 2, dates, LANES), F32),
            jax.ShapeDtypeStruct((2, chunks, rows, LANES), F32),
        ),
        in_specs=[vmem()] * 2,
        out_specs=[vmem()] * 4,
        scratch_shapes=[pltpu.VMEM((2, dates, LANES), F32)]
        + [pltpu.VMEM((rows * 2 * dates, band.shape[0]), BF16)] * group,
        compiler_params=params(),
        name="link_own",
    )(a, band)


def link_window(a, images, band, s, r, w, slots, paired):
    rows, chunks, dates, _ = r.shape
    scratch = [
        pltpu.VMEM((rows * 2 * (dates + SUB), band.shape[0]), BF16),
        pltpu.VMEM((slots, rows, chunks, 2, dates, LANES), F32),
        pltpu.VMEM((slots, rows, chunks, 2, SUB, LANES), F32),
        pltpu.VMEM((rows, chunks, SUB, LANES), F32),
        pltpu.VMEM((2, dates, LANES), F32),
        pltpu.VMEM((2, SUB, LANES), F32),
    ]
    if paired:
        scratch.append(pltpu.VMEM((3, 2, chunks, rows, LANES), F32))
    return pl.pallas_call(
        functools.partial(window_kernel, slots, paired),
        out_shape=jax.ShapeDtypeStruct((rows, chunks, 2, dates, LANES), F32),
        in_specs=[vmem()] * (5 + len(images)),
        out_specs=vmem(),
        scratch_shapes=scratch,
        compiler_params=params(),
        name="link_window",
    )(a, band, s, r, w, *images)


def swap(value, step):
    count = lax.axis_size("date")
    return lax.ppermute(value, "date", [(i, i ^ step) for i in range(count)])


def pick(cond, on_true, on_false):
    return jnp.where(cond, on_true, on_false)


def is_paired(x):
    return lax.axis_size("ms") == 2 and lax.axis_size("date") == 4 and x.shape[2] % (4 * SUB) == 0


def paired_windows(x):
    slabs = lax.axis_size("pix")
    block = block_of(lax.axis_index("date"), lax.axis_index("pix"))
    near = block < 2
    even = (block & 1) == 0
    lead = x.transpose(2, 0, 1, 3)
    rows = lead.shape[0] // 4
    reach = 2 * rows + HALF
    low, high = lead[:reach], lead[-reach:]
    own_pairs, far_pairs = [], []
    for date in range(4):
        for k in range(slabs):
            upper = block_of(date, k) < 2
            target = k - 1 if upper else k + 1
            inside = 0 <= target < slabs
            own_pairs.append((date * slabs + k, date * slabs + target if inside else (date ^ 1) * slabs + k))
            far_pairs.append(((date ^ 2) * slabs + (target if inside else k), date * slabs + k))
    outer = pick(near, lax.axis_index("pix") == 0, lax.axis_index("pix") == slabs - 1)
    top, bottom = lead[:HALF], lead[-HALF:]
    edge_own = lax.ppermute(pick(near, top, bottom), ("date", "pix"), own_pairs)
    edge_far = lax.ppermute(pick(near, bottom, top), ("date", "pix"), far_pairs)
    here = pick(near, low, high)
    far = swap(pick(near, high, low), 2)
    edge = jnp.concatenate([edge_own, edge_far], 2)
    edge = pick(outer, jnp.zeros_like(edge), edge)
    own = jnp.concatenate([here, far], 2)
    both = pick(near, jnp.concatenate([edge, own], 0), jnp.concatenate([own, edge], 0))
    tall = rows + 2 * HALF
    first, second = both[:tall], both[rows:]
    other = swap(pick(even, second, first), 1)
    return jnp.concatenate([pick(even, first, second), other], 2)


def plain_windows(x):
    count, slabs = lax.axis_size("date"), lax.axis_size("pix")
    me = lax.axis_index("date").astype(jnp.uint32)
    lead = x.transpose(2, 0, 1, 3)
    rows = lead.shape[0] // count
    tall = rows + 2 * HALF
    ups = [(k, k + 1) for k in range(slabs - 1)]
    downs = [(b, a) for a, b in ups]
    above = lax.ppermute(lead[-HALF:], "pix", ups)
    below = lax.ppermute(lead[:HALF], "pix", downs)
    padded = jnp.concatenate([above, lead, below], 0)

    def window(target):
        return lax.dynamic_slice_in_dim(padded, target * rows, tall, 0)

    parts = [window(me)] + [swap(window(me ^ step), step) for step in range(1, count)]
    return jnp.concatenate(parts, 2)


def earlier_windows(compressed, shift_by):
    stacks, count, slabs = lax.axis_size("ms"), lax.axis_size("date"), lax.axis_size("pix")
    rows = compressed.shape[1]
    reach = -(-HALF // rows)
    blocks = count * slabs

    def index(stack, block):
        k, d = divmod(block, count)
        return (stack * count + d) * slabs + k

    lead = compressed.transpose(1, 0, 2)
    parts = []
    for offset in range(-reach, reach + 1):
        low = max(0, -HALF - offset * rows)
        high = min(rows, rows + HALF - offset * rows)
        pairs = []
        for stack in range(stacks - shift_by):
            for block in range(blocks):
                target = block - offset
                if 0 <= target < blocks:
                    pairs.append((index(stack, block), index(stack + shift_by, target)))
        parts.append(lax.ppermute(lead[low:high], ("ms", "date", "pix"), pairs))
    return jnp.concatenate(parts, 0)


def assemble_kernel(offsets, *refs):
    date = lax.axis_index("date")
    block = block_of(date, lax.axis_index("pix"))
    pieces, (out_ref, mine_ref, whole_ref, sem) = refs[: len(offsets)], refs[len(offsets) :]
    own, rows = out_ref.shape[1], pieces[0].shape[2]
    copies = []
    for offset, piece in zip(offsets, pieces):
        row = pl.multiple_of((block ^ offset) * rows, rows)
        copy = pltpu.make_async_copy(
            piece.at[:, pl.ds(0, own)], out_ref.at[:, :, pl.ds(row, rows), :], sem.at[len(copies)]
        )
        copy.start()
        copies.append(copy)
        whole_ref[:, pl.ds(row, rows), :] = piece[:, own]
    width = mine_ref.shape[3]
    cols = whole_ref.shape[2]
    for c in range(2):
        rolled = pltpu.roll(whole_ref[c], lax.rem(cols - date * width, cols), 1)
        mine_ref[c, 0] = rolled[:, :width]
    for copy in copies:
        copy.wait()


def assemble(pieces, offsets, count):
    _, own, rows, cols = pieces[0].shape
    own = own - 1
    return pl.pallas_call(
        functools.partial(assemble_kernel, offsets),
        out_shape=(
            jax.ShapeDtypeStruct((2, own, rows * count, cols), F32),
            jax.ShapeDtypeStruct((2, 1, rows * count, cols // count), F32),
        ),
        in_specs=[vmem()] * len(pieces),
        out_specs=(pl.BlockSpec(memory_space=pl.ANY), vmem()),
        scratch_shapes=[pltpu.VMEM((2, rows * count, cols), F32), pltpu.SemaphoreType.DMA((len(pieces),))],
        compiler_params=params(8),
        name="assemble",
    )(*pieces)


def scatter(blocks, compressed, me, paired):
    count = lax.axis_size("date")
    _, own, rows, cols = blocks[0].shape
    if paired:
        image = compressed[:, None]
        mine, far, sibling, far_sibling = blocks
        got = swap(jnp.concatenate([far, far_sibling, image], 1), 2)
        to_send = jnp.stack(
            [jnp.concatenate([sibling, image], 1), got[:, own:]], 0
        )
        near = swap(to_send, 1)
        pieces = [
            jnp.concatenate([mine, image], 1),
            jnp.concatenate([got[:, :own], got[:, 2 * own :]], 1),
            near[0],
            near[1],
        ]
        return assemble(pieces, (0, 2, 1, 3), count)
    out = jnp.zeros((2, own + 1, rows * count, cols), F32)
    for step in range(count):
        piece = jnp.concatenate([blocks[step], compressed[:, None]], 1)
        piece = swap(piece, step) if step else piece
        out = lax.dynamic_update_slice_in_dim(out, piece, (me ^ step) * rows, 2)
    width = cols // count
    return (out[:, :own], lax.dynamic_slice_in_dim(out[:, own:], me * width, width, 3))


def earlier_images(compressed):
    slabs = lax.axis_size("pix")
    blocks = 4 * slabs

    def index(stack, block):
        k, t = divmod(block, 4)
        return (stack * 4 + block_of(t, k)) * slabs + k

    def crossing(block):
        target = block + 1 if block & 1 else block - 1
        return target if 0 <= target < blocks else block

    def move(target_of):
        pairs = [
            (index(stack, block), index(1 - stack, target_of(block))) for stack in range(2) for block in range(blocks)
        ]
        return lax.ppermute(compressed, ("ms", "date", "pix"), pairs)

    return [move(lambda block: block), move(lambda block: block ^ 1), move(crossing)]


def body(slc_stack):
    count = lax.axis_size("date")
    rows = slc_stack.shape[2] // count
    paired = is_paired(slc_stack)
    a = paired_windows(slc_stack) if paired else plain_windows(slc_stack)
    cols = a.shape[3]
    chunks = cols // LANES
    a = a.reshape(a.shape[:3] + (chunks, LANES)).transpose(0, 1, 3, 2, 4)
    places = jnp.arange(cols, dtype=jnp.int32)
    band = (jnp.abs(places[:, None] - places[None, :]) <= HALF).astype(BF16)
    band = jnp.concatenate([band, band], 0)
    me = lax.axis_index("date").astype(jnp.uint32)
    a, me = lax.optimization_barrier((a, me))
    s, r, w, compressed = link_own(a, band)
    slots = min(3, lax.axis_size("ms") - 1)
    image = compressed.transpose(0, 2, 1, 3).reshape(2, rows, cols)
    if paired:
        images = earlier_images(compressed)
    else:
        z = jnp.stack([earlier_windows(image, shift_by) for shift_by in range(1, slots + 1)], 2)
        z = jnp.pad(z, ((0, 0), (0, 0), (0, SUB - slots), (0, 0)))
        images = [z.reshape(z.shape[:3] + (chunks, LANES)).transpose(0, 1, 3, 2, 4)]
    linked = link_window(a, images, band, s, r, w, slots, paired)
    own = slc_stack.shape[1]
    blocks = [
        linked[:, :, :, j * own : (j + 1) * own].transpose(2, 3, 0, 1, 4).reshape(2, own, rows, cols)
        for j in range(count)
    ]
    return scatter(blocks, image, me, paired)


def solution(mesh):
    in_specs = (P(None, ("ms", "date"), "pix", None),)
    out_specs = (P(None, ("ms", "date"), "pix", None), P(None, "ms", "pix", "date"))
    return jax.shard_map(body, mesh=mesh, in_specs=in_specs, out_specs=out_specs, check_vma=False)
```

```python
import functools
import itertools
import math

import jax
import jax.numpy as jnp
from jax import lax
from jax.experimental import pallas as pl
from jax.experimental.pallas import tpu as pltpu
from jax.sharding import PartitionSpec as P

HALF = 5
ITERS = 3
WIDTH = 2 * HALF + 1
AREA = float(WIDTH**2)
EPSILON = 1e-06
SUB = 8
LANES = 128
TURNS = 2
F32 = jnp.float32
BF16 = jnp.bfloat16


def row_sums(values, count):
    suffix = [None] * WIDTH
    running = values[WIDTH - 1]
    suffix[WIDTH - 1] = running
    for row in range(WIDTH - 2, -1, -1):
        running = running + values[row]
        suffix[row] = running
    out = [suffix[0]]
    prefix = None
    for row in range(1, count):
        term = values[WIDTH - 1 + row]
        prefix = term if prefix is None else prefix + term
        out.append(suffix[row] + prefix)
    return out


def put_split(x_ref, at, chunk, value):
    high = value.astype(BF16)
    low = (value - high.astype(F32)).astype(BF16)
    total = x_ref.shape[1] // 2
    x_ref[pl.ds(at, value.shape[0]), pl.ds(chunk * LANES, LANES)] = high
    x_ref[pl.ds(at, value.shape[0]), pl.ds(total + chunk * LANES, LANES)] = low


def products(x_ref, blocks, other, rows, chunks):
    for chunk in range(chunks):
        for place, (ref, first) in enumerate(blocks):
            at = pl.ds(first, SUB)
            real, imag = [], []
            for row in range(rows + 2 * HALF):
                left_real, left_imag = ref[row, 0, chunk, at, :], ref[row, 1, chunk, at, :]
                right_real, right_imag = other(row, chunk)
                real.append(left_real * right_real + left_imag * right_imag)
                imag.append(left_imag * right_real - left_real * right_imag)
            sums = zip(row_sums(real, rows), row_sums(imag, rows))
            for row, both in enumerate(sums):
                put_split(x_ref, (row * len(blocks) + place) * 2 * SUB, chunk, jnp.concatenate(both, 0))


def energies(x_ref, ref, rows, chunks, dates):
    step = math.gcd(dates, 2 * SUB)
    for chunk in range(chunks):
        for first in range(0, dates, step):
            at = pl.ds(first, step)
            values = []
            for row in range(rows + 2 * HALF):
                real, imag = ref[row, 0, chunk, at, :], ref[row, 1, chunk, at, :]
                values.append(real * real + imag * imag)
            for row, total in enumerate(row_sums(values, rows)):
                put_split(x_ref, row * dates + first, chunk, total)


def across(x_ref, size, band_ref, chunk):
    band = band_ref[:, pl.ds(chunk * LANES, LANES)]
    return jnp.dot(x_ref[0:size, :], band, preferred_element_type=F32)


def spread(ref, *place):
    return ref[place[:-1] + (pl.ds(place[-1], SUB, stride=0), slice(None))]


def pitch(dates):
    return dates if (dates // SUB) % 2 else dates + SUB


def accumulate(total, term):
    return term if total is None else total + term


def matvec(s_ref, v_ref, base, dates):
    blocks = dates // SUB
    real, imag = [None] * blocks, [None] * blocks
    for q in range(dates):
        v_real, v_imag = spread(v_ref, 0, q), spread(v_ref, 1, q)
        for b in range(blocks):
            at = q * pitch(dates) + b * SUB
            s_real = s_ref[pl.ds(base + at, SUB), :]
            s_imag = s_ref[pl.ds(base + dates * pitch(dates) + at, SUB), :]
            real[b] = accumulate(real[b], s_real * v_real - s_imag * v_imag)
            imag[b] = accumulate(imag[b], s_real * v_imag + s_imag * v_real)
    return jnp.concatenate(real, 0), jnp.concatenate(imag, 0)


def fill_and_apply(s_ref, v_ref, base, dates):
    blocks = dates // SUB
    real, imag = [None] * blocks, [None] * blocks
    half = dates * pitch(dates)
    for q in range(dates):
        v_real = spread(v_ref, 0, q)
        for b in range(blocks):
            at = pl.ds(base + q * pitch(dates) + b * SUB, SUB)
            at_imag = pl.ds(base + half + q * pitch(dates) + b * SUB, SUB)
            if b < q // SUB:
                turned = base + b * SUB * pitch(dates) + q
                s_real = s_ref[pl.ds(turned, SUB, stride=pitch(dates)), :]
                s_imag = -s_ref[pl.ds(turned + half, SUB, stride=pitch(dates)), :]
                s_ref[at, :] = s_real
                s_ref[at_imag, :] = s_imag
            else:
                s_real, s_imag = s_ref[at, :], s_ref[at_imag, :]
            real[b] = accumulate(real[b], s_real * v_real)
            imag[b] = accumulate(imag[b], s_imag * v_real)
    return jnp.concatenate(real, 0), jnp.concatenate(imag, 0)


def total_square(real, imag):
    return jnp.sum(real * real + imag * imag, axis=0, keepdims=True)


def each_row(rows, chunks, one_row):
    turns = math.gcd(rows, TURNS)
    for chunk in range(chunks):

        def together(step, carry, chunk=chunk):
            running = [one_row(chunk, step * turns + turn, turn) for turn in range(turns)]
            for _ in itertools.zip_longest(*running):
                pass
            return carry

        lax.fori_loop(0, rows // turns, together, 0)


def own_kernel(a_ref, band_ref, s_ref, r_ref, w_ref, comp_ref, v_ref, *x_refs):
    rows, chunks, dates, _ = r_ref.shape
    blocks = dates // SUB
    half = dates * pitch(dates)
    group = len(x_refs)

    energies(x_refs[0], a_ref, rows, chunks, dates)
    for chunk in range(chunks):
        power = across(x_refs[0], rows * dates, band_ref, chunk)
        scale = lax.rsqrt(power / AREA + EPSILON)
        r_ref[:, chunk] = scale.reshape(rows, dates, LANES)

    for q_block in range(blocks):
        kept = [(a_ref, b * SUB) for b in range(q_block, blocks)]

        def one_group(turn, carry, q_block=q_block, kept=kept):
            for u in range(group):
                q = q_block * SUB + turn * group + u

                def other(row, chunk, q=q):
                    return spread(a_ref, row, 0, chunk, q), spread(a_ref, row, 1, chunk, q)

                products(x_refs[u], kept, other, rows, chunks)
                for chunk in range(chunks):
                    summed = across(x_refs[u], rows * len(kept) * 2 * SUB, band_ref, chunk)
                    for row in range(rows):
                        for place, (_, first) in enumerate(kept):
                            for c in range(2):
                                value = summed[((row * len(kept) + place) * 2 + c) * SUB :][:SUB]
                                at = (row * chunks + chunk) * 2 * half + c * half + q * pitch(dates) + first
                                s_ref[pl.ds(pl.multiple_of(at, SUB), SUB), :] = value
            return carry

        lax.fori_loop(0, SUB // group, one_group, 0)

    def one_row(chunk, row, turn):
        v = v_ref.at[turn]
        base = pl.multiple_of((row * chunks + chunk) * 2 * half, SUB)
        scale = r_ref[row, chunk]
        v[0] = scale
        for repeat in range(ITERS):
            if repeat == 0:
                real, imag = fill_and_apply(s_ref, v, base, dates)
            else:
                real, imag = matvec(s_ref, v, base, dates)
            real, imag = real * (scale / AREA), imag * (scale / AREA)
            if repeat == 0:
                w_ref[row, chunk, 0] = real
                w_ref[row, chunk, 1] = imag
            factor = lax.rsqrt(total_square(real, imag) / dates + EPSILON)
            real, imag = real * factor, imag * factor
            if repeat < ITERS - 1:
                v[0] = real * scale
                v[1] = imag * scale
            yield
        centre_real, centre_imag = a_ref[row + HALF, 0, chunk], a_ref[row + HALF, 1, chunk]
        root = math.sqrt(dates)
        comp_real = jnp.sum(real * centre_real + imag * centre_imag, axis=0, keepdims=True)
        comp_imag = jnp.sum(real * centre_imag - imag * centre_real, axis=0, keepdims=True)
        comp_ref[0, chunk, pl.ds(row, 1), :] = comp_real / root
        comp_ref[1, chunk, pl.ds(row, 1), :] = comp_imag / root

    each_row(rows, chunks, one_row)


def block_of(date, slab):
    return date ^ (2 * (slab & 1))


def fill_window(z_ref, images):
    centre_ref, sibling_ref, other_ref = images
    slab, slabs = lax.axis_index("pix"), lax.axis_size("pix")
    block = block_of(lax.axis_index("date"), slab)
    even = (block & 1) == 0
    known = lax.axis_index("ms") > 0
    inner = known & jnp.logical_not(((slab == 0) & (block == 0)) | ((slab == slabs - 1) & (block == 3)))
    sibling = jnp.where(known, sibling_ref[...], 0.0)
    other = jnp.where(inner, other_ref[...], 0.0)
    z_ref[0] = jnp.where(even, other, sibling)
    z_ref[1] = jnp.where(known, centre_ref[...], 0.0)
    z_ref[2] = jnp.where(even, sibling, other)


class Row:
    def __init__(self, z_ref, rows):
        self.z_ref, self.rows = z_ref, rows

    def __getitem__(self, index):
        row, c, chunk = index[:3]
        part, at = divmod(row - HALF + self.rows, self.rows)
        return spread(self.z_ref, part, c, chunk, at)


def window_kernel(slots, paired, *refs):
    a_ref, band_ref, s_ref, r_ref, w_ref = refs[:5]
    rows, chunks, dates, _ = r_ref.shape
    count = 3 if paired else 1
    images = refs[5 : 5 + count]
    out_ref, x_ref, m_ref, zz_ref, rz_ref, v_ref, vz_ref = refs[5 + count : 12 + count]
    blocks = dates // SUB
    half = dates * pitch(dates)
    if paired:
        fill_window(refs[12 + count], images)
        z = Row(refs[12 + count], rows)
    else:
        z = images[0]
        energies(x_ref, z, rows, chunks, SUB)
        for chunk in range(chunks):
            power = across(x_ref, rows * SUB, band_ref, chunk)
            rz_ref[:, chunk] = lax.rsqrt(power / AREA + EPSILON).reshape(rows, SUB, LANES)

    kept = [(a_ref, b * SUB) for b in range(blocks)] + [(z, 0)]
    for slot in range(slots):

        def other(row, chunk, slot=slot):
            if paired:
                return z[row, 0, chunk], z[row, 1, chunk]
            return spread(z, row, 0, chunk, slot), spread(z, row, 1, chunk, slot)

        products(x_ref, kept, other, rows, chunks)
        for chunk in range(chunks):
            summed = across(x_ref, rows * len(kept) * 2 * SUB, band_ref, chunk)
            for row in range(rows):
                for place, (_, first) in enumerate(kept):
                    for c in range(2):
                        value = summed[((row * len(kept) + place) * 2 + c) * SUB :][:SUB]
                        if place < blocks:
                            m_ref[slot, row, chunk, c, pl.ds(first, SUB), :] = value
                        else:
                            zz_ref[slot, row, chunk, c] = value
                            if paired and c == 0:
                                rz_ref[row, chunk] = lax.rsqrt(value / AREA + EPSILON)

    place = lax.broadcasted_iota(jnp.int32, (SUB, LANES), 0)

    def one_row(chunk, row, turn):
        v, vz = v_ref.at[turn], vz_ref.at[turn]
        base = pl.multiple_of((row * chunks + chunk) * 2 * half, SUB)
        scale = r_ref[row, chunk]
        scale_z = rz_ref[row, chunk]
        v[0] = scale
        v[1] = jnp.zeros_like(scale)
        vz[0] = scale_z
        vz[1] = jnp.zeros_like(scale_z)
        for repeat in range(ITERS):
            if repeat == 0:
                real, imag = w_ref[row, chunk, 0], w_ref[row, chunk, 1]
            else:
                real, imag = matvec(s_ref, v, base, dates)
                real, imag = real * (scale / AREA), imag * (scale / AREA)
            add_real, add_imag = jnp.zeros_like(real), jnp.zeros_like(imag)
            z_real, z_imag = jnp.zeros_like(scale_z), jnp.zeros_like(scale_z)
            old_real, old_imag = v[0], v[1]
            for slot in range(slots):
                v_real, v_imag = vz[0, pl.ds(slot, 1), :], vz[1, pl.ds(slot, 1), :]
                m_real, m_imag = m_ref[slot, row, chunk, 0], m_ref[slot, row, chunk, 1]
                add_real = add_real + m_real * v_real - m_imag * v_imag
                add_imag = add_imag + m_real * v_imag + m_imag * v_real
                sum_real = jnp.sum(m_real * old_real + m_imag * old_imag, axis=0, keepdims=True)
                sum_imag = jnp.sum(m_real * old_imag - m_imag * old_real, axis=0, keepdims=True)
                z_real = z_real + jnp.where(place == slot, sum_real, 0.0)
                z_imag = z_imag + jnp.where(place == slot, sum_imag, 0.0)
                zz_real, zz_imag = zz_ref[slot, row, chunk, 0], zz_ref[slot, row, chunk, 1]
                z_real = z_real + zz_real * v_real - zz_imag * v_imag
                z_imag = z_imag + zz_real * v_imag + zz_imag * v_real
            real = real + add_real * (scale / AREA)
            imag = imag + add_imag * (scale / AREA)
            z_real = jnp.where(place < slots, z_real * (scale_z / AREA), 0.0)
            z_imag = jnp.where(place < slots, z_imag * (scale_z / AREA), 0.0)
            square = total_square(real, imag) + total_square(z_real, z_imag)
            factor = lax.rsqrt(square / (slots + dates) + EPSILON)
            real, imag = real * factor, imag * factor
            if repeat < ITERS - 1:
                v[0] = real * scale
                v[1] = imag * scale
                vz[0] = z_real * factor * scale_z
                vz[1] = z_imag * factor * scale_z
            yield
        out_ref[row, chunk, 0] = real
        out_ref[row, chunk, 1] = imag

    each_row(rows, chunks, one_row)


def vmem():
    return pl.BlockSpec(memory_space=pltpu.VMEM)


def params(limit=24):
    return pltpu.CompilerParams(vmem_limit_bytes=limit * 2**20)


def link_own(a, band, group=8):
    rows, chunks, dates = a.shape[0] - 2 * HALF, a.shape[2], a.shape[3]
    return pl.pallas_call(
        own_kernel,
        out_shape=(
            jax.ShapeDtypeStruct((rows * chunks * 2 * dates * pitch(dates), LANES), F32),
            jax.ShapeDtypeStruct((rows, chunks, dates, LANES), F32),
            jax.ShapeDtypeStruct((rows, chunks, 2, dates, LANES), F32),
            jax.ShapeDtypeStruct((2, chunks, rows, LANES), F32),
        ),
        in_specs=[vmem()] * 2,
        out_specs=[vmem()] * 4,
        scratch_shapes=[pltpu.VMEM((TURNS, 2, dates, LANES), F32)]
        + [pltpu.VMEM((rows * 2 * dates, band.shape[0]), BF16)] * group,
        compiler_params=params(),
        name="link_own",
    )(a, band)


def link_window(a, images, band, s, r, w, slots, paired):
    rows, chunks, dates, _ = r.shape
    scratch = [
        pltpu.VMEM((rows * 2 * (dates + SUB), band.shape[0]), BF16),
        pltpu.VMEM((slots, rows, chunks, 2, dates, LANES), F32),
        pltpu.VMEM((slots, rows, chunks, 2, SUB, LANES), F32),
        pltpu.VMEM((rows, chunks, SUB, LANES), F32),
        pltpu.VMEM((TURNS, 2, dates, LANES), F32),
        pltpu.VMEM((TURNS, 2, SUB, LANES), F32),
    ]
    if paired:
        scratch.append(pltpu.VMEM((3, 2, chunks, rows, LANES), F32))
    return pl.pallas_call(
        functools.partial(window_kernel, slots, paired),
        out_shape=jax.ShapeDtypeStruct((rows, chunks, 2, dates, LANES), F32),
        in_specs=[vmem()] * (5 + len(images)),
        out_specs=vmem(),
        scratch_shapes=scratch,
        compiler_params=params(),
        name="link_window",
    )(a, band, s, r, w, *images)


def swap(value, step):
    count = lax.axis_size("date")
    return lax.ppermute(value, "date", [(i, i ^ step) for i in range(count)])


def pick(cond, on_true, on_false):
    return jnp.where(cond, on_true, on_false)


def is_paired(x):
    return lax.axis_size("ms") == 2 and lax.axis_size("date") == 4 and x.shape[2] % (4 * SUB) == 0


def paired_windows(x):
    slabs = lax.axis_size("pix")
    block = block_of(lax.axis_index("date"), lax.axis_index("pix"))
    near = block < 2
    even = (block & 1) == 0
    lead = x.transpose(2, 0, 1, 3)
    rows = lead.shape[0] // 4
    reach = 2 * rows + HALF
    low, high = lead[:reach], lead[-reach:]
    own_pairs, far_pairs = [], []
    for date in range(4):
        for k in range(slabs):
            upper = block_of(date, k) < 2
            target = k - 1 if upper else k + 1
            inside = 0 <= target < slabs
            own_pairs.append((date * slabs + k, date * slabs + target if inside else (date ^ 1) * slabs + k))
            far_pairs.append(((date ^ 2) * slabs + (target if inside else k), date * slabs + k))
    outer = pick(near, lax.axis_index("pix") == 0, lax.axis_index("pix") == slabs - 1)
    top, bottom = lead[:HALF], lead[-HALF:]
    edge_own = lax.ppermute(pick(near, top, bottom), ("date", "pix"), own_pairs)
    edge_far = lax.ppermute(pick(near, bottom, top), ("date", "pix"), far_pairs)
    here = pick(near, low, high)
    far = swap(pick(near, high, low), 2)
    edge = jnp.concatenate([edge_own, edge_far], 2)
    edge = pick(outer, jnp.zeros_like(edge), edge)
    own = jnp.concatenate([here, far], 2)
    both = pick(near, jnp.concatenate([edge, own], 0), jnp.concatenate([own, edge], 0))
    tall = rows + 2 * HALF
    first, second = both[:tall], both[rows:]
    other = swap(pick(even, second, first), 1)
    return jnp.concatenate([pick(even, first, second), other], 2)


def plain_windows(x):
    count, slabs = lax.axis_size("date"), lax.axis_size("pix")
    me = lax.axis_index("date").astype(jnp.uint32)
    lead = x.transpose(2, 0, 1, 3)
    rows = lead.shape[0] // count
    tall = rows + 2 * HALF
    ups = [(k, k + 1) for k in range(slabs - 1)]
    downs = [(b, a) for a, b in ups]
    above = lax.ppermute(lead[-HALF:], "pix", ups)
    below = lax.ppermute(lead[:HALF], "pix", downs)
    padded = jnp.concatenate([above, lead, below], 0)

    def window(target):
        return lax.dynamic_slice_in_dim(padded, target * rows, tall, 0)

    parts = [window(me)] + [swap(window(me ^ step), step) for step in range(1, count)]
    return jnp.concatenate(parts, 2)


def earlier_windows(compressed, shift_by):
    stacks, count, slabs = lax.axis_size("ms"), lax.axis_size("date"), lax.axis_size("pix")
    rows = compressed.shape[1]
    reach = -(-HALF // rows)
    blocks = count * slabs

    def index(stack, block):
        k, d = divmod(block, count)
        return (stack * count + d) * slabs + k

    lead = compressed.transpose(1, 0, 2)
    parts = []
    for offset in range(-reach, reach + 1):
        low = max(0, -HALF - offset * rows)
        high = min(rows, rows + HALF - offset * rows)
        pairs = []
        for stack in range(stacks - shift_by):
            for block in range(blocks):
                target = block - offset
                if 0 <= target < blocks:
                    pairs.append((index(stack, block), index(stack + shift_by, target)))
        parts.append(lax.ppermute(lead[low:high], ("ms", "date", "pix"), pairs))
    return jnp.concatenate(parts, 0)


def assemble_kernel(offsets, *refs):
    date = lax.axis_index("date")
    block = block_of(date, lax.axis_index("pix"))
    pieces, (out_ref, mine_ref, whole_ref, sem) = refs[: len(offsets)], refs[len(offsets) :]
    own, rows = out_ref.shape[1], pieces[0].shape[2]
    copies = []
    for offset, piece in zip(offsets, pieces):
        row = pl.multiple_of((block ^ offset) * rows, rows)
        copy = pltpu.make_async_copy(
            piece.at[:, pl.ds(0, own)], out_ref.at[:, :, pl.ds(row, rows), :], sem.at[len(copies)]
        )
        copy.start()
        copies.append(copy)
        whole_ref[:, pl.ds(row, rows), :] = piece[:, own]
    width = mine_ref.shape[3]
    cols = whole_ref.shape[2]
    for c in range(2):
        rolled = pltpu.roll(whole_ref[c], lax.rem(cols - date * width, cols), 1)
        mine_ref[c, 0] = rolled[:, :width]
    for copy in copies:
        copy.wait()


def assemble(pieces, offsets, count):
    _, own, rows, cols = pieces[0].shape
    own = own - 1
    return pl.pallas_call(
        functools.partial(assemble_kernel, offsets),
        out_shape=(
            jax.ShapeDtypeStruct((2, own, rows * count, cols), F32),
            jax.ShapeDtypeStruct((2, 1, rows * count, cols // count), F32),
        ),
        in_specs=[vmem()] * len(pieces),
        out_specs=(pl.BlockSpec(memory_space=pl.ANY), vmem()),
        scratch_shapes=[pltpu.VMEM((2, rows * count, cols), F32), pltpu.SemaphoreType.DMA((len(pieces),))],
        compiler_params=params(8),
        name="assemble",
    )(*pieces)


def scatter(blocks, compressed, me, paired):
    count = lax.axis_size("date")
    _, own, rows, cols = blocks[0].shape
    if paired:
        image = compressed[:, None]
        mine, far, sibling, far_sibling = blocks
        got = swap(jnp.concatenate([far, far_sibling, image], 1), 2)
        to_send = jnp.stack(
            [jnp.concatenate([sibling, image], 1), got[:, own:]], 0
        )
        near = swap(to_send, 1)
        pieces = [
            jnp.concatenate([mine, image], 1),
            jnp.concatenate([got[:, :own], got[:, 2 * own :]], 1),
            near[0],
            near[1],
        ]
        return assemble(pieces, (0, 2, 1, 3), count)
    out = jnp.zeros((2, own + 1, rows * count, cols), F32)
    for step in range(count):
        piece = jnp.concatenate([blocks[step], compressed[:, None]], 1)
        piece = swap(piece, step) if step else piece
        out = lax.dynamic_update_slice_in_dim(out, piece, (me ^ step) * rows, 2)
    width = cols // count
    return (out[:, :own], lax.dynamic_slice_in_dim(out[:, own:], me * width, width, 3))


def earlier_images(compressed):
    slabs = lax.axis_size("pix")
    blocks = 4 * slabs

    def index(stack, block):
        k, t = divmod(block, 4)
        return (stack * 4 + block_of(t, k)) * slabs + k

    def crossing(block):
        target = block + 1 if block & 1 else block - 1
        return target if 0 <= target < blocks else block

    def move(target_of):
        pairs = [
            (index(stack, block), index(1 - stack, target_of(block))) for stack in range(2) for block in range(blocks)
        ]
        return lax.ppermute(compressed, ("ms", "date", "pix"), pairs)

    return [move(lambda block: block), move(lambda block: block ^ 1), move(crossing)]


def body(slc_stack):
    count = lax.axis_size("date")
    rows = slc_stack.shape[2] // count
    paired = is_paired(slc_stack)
    a = paired_windows(slc_stack) if paired else plain_windows(slc_stack)
    cols = a.shape[3]
    chunks = cols // LANES
    a = a.reshape(a.shape[:3] + (chunks, LANES)).transpose(0, 1, 3, 2, 4)
    places = jnp.arange(cols, dtype=jnp.int32)
    band = (jnp.abs(places[:, None] - places[None, :]) <= HALF).astype(BF16)
    band = jnp.concatenate([band, band], 0)
    me = lax.axis_index("date").astype(jnp.uint32)
    a, me = lax.optimization_barrier((a, me))
    s, r, w, compressed = link_own(a, band)
    slots = min(3, lax.axis_size("ms") - 1)
    image = compressed.transpose(0, 2, 1, 3).reshape(2, rows, cols)
    if paired:
        images = earlier_images(compressed)
    else:
        z = jnp.stack([earlier_windows(image, shift_by) for shift_by in range(1, slots + 1)], 2)
        z = jnp.pad(z, ((0, 0), (0, 0), (0, SUB - slots), (0, 0)))
        images = [z.reshape(z.shape[:3] + (chunks, LANES)).transpose(0, 1, 3, 2, 4)]
    linked = link_window(a, images, band, s, r, w, slots, paired)
    own = slc_stack.shape[1]
    blocks = [
        linked[:, :, :, j * own : (j + 1) * own].transpose(2, 3, 0, 1, 4).reshape(2, own, rows, cols)
        for j in range(count)
    ]
    return scatter(blocks, image, me, paired)


def solution(mesh):
    in_specs = (P(None, ("ms", "date"), "pix", None),)
    out_specs = (P(None, ("ms", "date"), "pix", None), P(None, "ms", "pix", "date"))
    return jax.shard_map(body, mesh=mesh, in_specs=in_specs, out_specs=out_specs, check_vma=False)
```

```python
import functools
import itertools
import math

import jax
import jax.numpy as jnp
from jax import lax
from jax.experimental import pallas as pl
from jax.experimental.pallas import tpu as pltpu
from jax.sharding import PartitionSpec as P

HALF = 5
ITERS = 3
WIDTH = 2 * HALF + 1
AREA = float(WIDTH**2)
EPSILON = 1e-06
SUB = 8
LANES = 128
TURNS = 2
F32 = jnp.float32
BF16 = jnp.bfloat16


def row_sums(values, count):
    suffix = [None] * WIDTH
    running = values[WIDTH - 1]
    suffix[WIDTH - 1] = running
    for row in range(WIDTH - 2, -1, -1):
        running = running + values[row]
        suffix[row] = running
    out = [suffix[0]]
    prefix = None
    for row in range(1, count):
        term = values[WIDTH - 1 + row]
        prefix = term if prefix is None else prefix + term
        out.append(suffix[row] + prefix)
    return out


def put_split(x_ref, at, chunk, value):
    high = value.astype(BF16)
    low = (value - high.astype(F32)).astype(BF16)
    total = x_ref.shape[1] // 2
    x_ref[pl.ds(at, value.shape[0]), pl.ds(chunk * LANES, LANES)] = high
    x_ref[pl.ds(at, value.shape[0]), pl.ds(total + chunk * LANES, LANES)] = low


def products(x_ref, blocks, other, rows, chunks):
    for chunk in range(chunks):
        for place, (ref, first) in enumerate(blocks):
            at = pl.ds(first, SUB)
            real, imag = [], []
            for row in range(rows + 2 * HALF):
                left_real, left_imag = ref[row, 0, chunk, at, :], ref[row, 1, chunk, at, :]
                right_real, right_imag = other(row, chunk)
                real.append(left_real * right_real + left_imag * right_imag)
                imag.append(left_imag * right_real - left_real * right_imag)
            sums = zip(row_sums(real, rows), row_sums(imag, rows))
            for row, both in enumerate(sums):
                put_split(x_ref, (row * len(blocks) + place) * 2 * SUB, chunk, jnp.concatenate(both, 0))


def energies(x_ref, ref, rows, chunks, dates):
    step = math.gcd(dates, 2 * SUB)
    for chunk in range(chunks):
        for first in range(0, dates, step):
            at = pl.ds(first, step)
            values = []
            for row in range(rows + 2 * HALF):
                real, imag = ref[row, 0, chunk, at, :], ref[row, 1, chunk, at, :]
                values.append(real * real + imag * imag)
            for row, total in enumerate(row_sums(values, rows)):
                put_split(x_ref, row * dates + first, chunk, total)


def across(x_ref, size, band_ref, chunk):
    band = band_ref[:, pl.ds(chunk * LANES, LANES)]
    return jnp.dot(x_ref[0:size, :], band, preferred_element_type=F32)


def spread(ref, *place):
    return ref[place[:-1] + (pl.ds(place[-1], SUB, stride=0), slice(None))]


def pitch(dates):
    return dates if (dates // SUB) % 2 else dates + SUB


def accumulate(total, term):
    return term if total is None else total + term


def matvec(s_ref, v_ref, base, dates):
    blocks = dates // SUB
    real, imag = [None] * blocks, [None] * blocks
    for q in range(dates):
        v_real, v_imag = spread(v_ref, 0, q), spread(v_ref, 1, q)
        for b in range(blocks):
            at = q * pitch(dates) + b * SUB
            s_real = s_ref[pl.ds(base + at, SUB), :]
            s_imag = s_ref[pl.ds(base + dates * pitch(dates) + at, SUB), :]
            real[b] = accumulate(real[b], s_real * v_real - s_imag * v_imag)
            imag[b] = accumulate(imag[b], s_real * v_imag + s_imag * v_real)
    return jnp.concatenate(real, 0), jnp.concatenate(imag, 0)


def fill_and_apply(s_ref, v_ref, base, dates):
    blocks = dates // SUB
    real, imag = [None] * blocks, [None] * blocks
    half = dates * pitch(dates)
    for q in range(dates):
        v_real = spread(v_ref, 0, q)
        for b in range(blocks):
            at = pl.ds(base + q * pitch(dates) + b * SUB, SUB)
            at_imag = pl.ds(base + half + q * pitch(dates) + b * SUB, SUB)
            if b < q // SUB:
                turned = base + b * SUB * pitch(dates) + q
                s_real = s_ref[pl.ds(turned, SUB, stride=pitch(dates)), :]
                s_imag = -s_ref[pl.ds(turned + half, SUB, stride=pitch(dates)), :]
                s_ref[at, :] = s_real
                s_ref[at_imag, :] = s_imag
            else:
                s_real, s_imag = s_ref[at, :], s_ref[at_imag, :]
            real[b] = accumulate(real[b], s_real * v_real)
            imag[b] = accumulate(imag[b], s_imag * v_real)
    return jnp.concatenate(real, 0), jnp.concatenate(imag, 0)


def total_square(real, imag):
    return jnp.sum(real * real + imag * imag, axis=0, keepdims=True)


def each_row(rows, chunks, one_row):
    turns = math.gcd(rows, TURNS)
    for chunk in range(chunks):

        def together(step, carry, chunk=chunk):
            running = [one_row(chunk, step * turns + turn, turn) for turn in range(turns)]
            for _ in itertools.zip_longest(*running):
                pass
            return carry

        lax.fori_loop(0, rows // turns, together, 0)


def own_kernel(a_ref, band_ref, s_ref, r_ref, w_ref, comp_ref, v_ref, *x_refs):
    rows, chunks, dates, _ = r_ref.shape
    blocks = dates // SUB
    half = dates * pitch(dates)
    group = len(x_refs)

    for q_block in range(blocks):
        kept = [(a_ref, b * SUB) for b in range(q_block, blocks)]

        def one_group(turn, carry, q_block=q_block, kept=kept):
            for u in range(group):
                q = q_block * SUB + turn * group + u

                def other(row, chunk, q=q):
                    return spread(a_ref, row, 0, chunk, q), spread(a_ref, row, 1, chunk, q)

                products(x_refs[u], kept, other, rows, chunks)
                for chunk in range(chunks):
                    summed = across(x_refs[u], rows * len(kept) * 2 * SUB, band_ref, chunk)
                    for row in range(rows):
                        for place, (_, first) in enumerate(kept):
                            for c in range(2):
                                value = summed[((row * len(kept) + place) * 2 + c) * SUB :][:SUB]
                                at = (row * chunks + chunk) * 2 * half + c * half + q * pitch(dates) + first
                                s_ref[pl.ds(pl.multiple_of(at, SUB), SUB), :] = value
            return carry

        lax.fori_loop(0, SUB // group, one_group, 0)

    def one_row(chunk, row, turn):
        v = v_ref.at[turn]
        base = pl.multiple_of((row * chunks + chunk) * 2 * half, SUB)
        step = pitch(dates) + 1
        power = [s_ref[pl.ds(base + b * SUB * step, SUB, stride=step), :] for b in range(blocks)]
        scale = lax.rsqrt(jnp.concatenate(power, 0) / AREA + EPSILON)
        r_ref[row, chunk] = scale
        v[0] = scale
        for repeat in range(ITERS):
            if repeat == 0:
                real, imag = fill_and_apply(s_ref, v, base, dates)
            else:
                real, imag = matvec(s_ref, v, base, dates)
            real, imag = real * (scale / AREA), imag * (scale / AREA)
            if repeat == 0:
                w_ref[row, chunk, 0] = real
                w_ref[row, chunk, 1] = imag
            factor = lax.rsqrt(total_square(real, imag) / dates + EPSILON)
            real, imag = real * factor, imag * factor
            if repeat < ITERS - 1:
                v[0] = real * scale
                v[1] = imag * scale
            yield
        centre_real, centre_imag = a_ref[row + HALF, 0, chunk], a_ref[row + HALF, 1, chunk]
        root = math.sqrt(dates)
        comp_real = jnp.sum(real * centre_real + imag * centre_imag, axis=0, keepdims=True)
        comp_imag = jnp.sum(real * centre_imag - imag * centre_real, axis=0, keepdims=True)
        comp_ref[0, chunk, pl.ds(row, 1), :] = comp_real / root
        comp_ref[1, chunk, pl.ds(row, 1), :] = comp_imag / root

    each_row(rows, chunks, one_row)


def block_of(date, slab):
    return date ^ (2 * (slab & 1))


def fill_window(z_ref, images):
    centre_ref, sibling_ref, other_ref = images
    slab, slabs = lax.axis_index("pix"), lax.axis_size("pix")
    block = block_of(lax.axis_index("date"), slab)
    even = (block & 1) == 0
    known = lax.axis_index("ms") > 0
    inner = known & jnp.logical_not(((slab == 0) & (block == 0)) | ((slab == slabs - 1) & (block == 3)))
    sibling = jnp.where(known, sibling_ref[...], 0.0)
    other = jnp.where(inner, other_ref[...], 0.0)
    z_ref[0] = jnp.where(even, other, sibling)
    z_ref[1] = jnp.where(known, centre_ref[...], 0.0)
    z_ref[2] = jnp.where(even, sibling, other)


class Row:
    def __init__(self, z_ref, rows):
        self.z_ref, self.rows = z_ref, rows

    def __getitem__(self, index):
        row, c, chunk = index[:3]
        part, at = divmod(row - HALF + self.rows, self.rows)
        return spread(self.z_ref, part, c, chunk, at)


def window_kernel(slots, paired, *refs):
    a_ref, band_ref, s_ref, r_ref, w_ref = refs[:5]
    rows, chunks, dates, _ = r_ref.shape
    count = 3 if paired else 1
    images = refs[5 : 5 + count]
    out_ref, x_ref, m_ref, zz_ref, rz_ref, v_ref, vz_ref = refs[5 + count : 12 + count]
    blocks = dates // SUB
    half = dates * pitch(dates)
    if paired:
        fill_window(refs[12 + count], images)
        z = Row(refs[12 + count], rows)
    else:
        z = images[0]
        energies(x_ref, z, rows, chunks, SUB)
        for chunk in range(chunks):
            power = across(x_ref, rows * SUB, band_ref, chunk)
            rz_ref[:, chunk] = lax.rsqrt(power / AREA + EPSILON).reshape(rows, SUB, LANES)

    kept = [(a_ref, b * SUB) for b in range(blocks)] + [(z, 0)]
    for slot in range(slots):

        def other(row, chunk, slot=slot):
            if paired:
                return z[row, 0, chunk], z[row, 1, chunk]
            return spread(z, row, 0, chunk, slot), spread(z, row, 1, chunk, slot)

        products(x_ref, kept, other, rows, chunks)
        for chunk in range(chunks):
            summed = across(x_ref, rows * len(kept) * 2 * SUB, band_ref, chunk)
            for row in range(rows):
                for place, (_, first) in enumerate(kept):
                    for c in range(2):
                        value = summed[((row * len(kept) + place) * 2 + c) * SUB :][:SUB]
                        if place < blocks:
                            m_ref[slot, row, chunk, c, pl.ds(first, SUB), :] = value
                        else:
                            zz_ref[slot, row, chunk, c] = value
                            if paired and c == 0:
                                rz_ref[row, chunk] = lax.rsqrt(value / AREA + EPSILON)

    place = lax.broadcasted_iota(jnp.int32, (SUB, LANES), 0)

    def one_row(chunk, row, turn):
        v, vz = v_ref.at[turn], vz_ref.at[turn]
        base = pl.multiple_of((row * chunks + chunk) * 2 * half, SUB)
        scale = r_ref[row, chunk]
        scale_z = rz_ref[row, chunk]
        v[0] = scale
        v[1] = jnp.zeros_like(scale)
        vz[0] = scale_z
        vz[1] = jnp.zeros_like(scale_z)
        for repeat in range(ITERS):
            if repeat == 0:
                real, imag = w_ref[row, chunk, 0], w_ref[row, chunk, 1]
            else:
                real, imag = matvec(s_ref, v, base, dates)
                real, imag = real * (scale / AREA), imag * (scale / AREA)
            add_real, add_imag = jnp.zeros_like(real), jnp.zeros_like(imag)
            z_real, z_imag = jnp.zeros_like(scale_z), jnp.zeros_like(scale_z)
            old_real, old_imag = v[0], v[1]
            for slot in range(slots):
                v_real, v_imag = vz[0, pl.ds(slot, 1), :], vz[1, pl.ds(slot, 1), :]
                m_real, m_imag = m_ref[slot, row, chunk, 0], m_ref[slot, row, chunk, 1]
                add_real = add_real + m_real * v_real - m_imag * v_imag
                add_imag = add_imag + m_real * v_imag + m_imag * v_real
                sum_real = jnp.sum(m_real * old_real + m_imag * old_imag, axis=0, keepdims=True)
                sum_imag = jnp.sum(m_real * old_imag - m_imag * old_real, axis=0, keepdims=True)
                z_real = z_real + jnp.where(place == slot, sum_real, 0.0)
                z_imag = z_imag + jnp.where(place == slot, sum_imag, 0.0)
                zz_real, zz_imag = zz_ref[slot, row, chunk, 0], zz_ref[slot, row, chunk, 1]
                z_real = z_real + zz_real * v_real - zz_imag * v_imag
                z_imag = z_imag + zz_real * v_imag + zz_imag * v_real
            real = real + add_real * (scale / AREA)
            imag = imag + add_imag * (scale / AREA)
            z_real = jnp.where(place < slots, z_real * (scale_z / AREA), 0.0)
            z_imag = jnp.where(place < slots, z_imag * (scale_z / AREA), 0.0)
            square = total_square(real, imag) + total_square(z_real, z_imag)
            factor = lax.rsqrt(square / (slots + dates) + EPSILON)
            real, imag = real * factor, imag * factor
            if repeat < ITERS - 1:
                v[0] = real * scale
                v[1] = imag * scale
                vz[0] = z_real * factor * scale_z
                vz[1] = z_imag * factor * scale_z
            yield
        out_ref[row, chunk, 0] = real
        out_ref[row, chunk, 1] = imag

    each_row(rows, chunks, one_row)


def vmem():
    return pl.BlockSpec(memory_space=pltpu.VMEM)


def params(limit=24):
    return pltpu.CompilerParams(vmem_limit_bytes=limit * 2**20)


def link_own(a, band, group=8):
    rows, chunks, dates = a.shape[0] - 2 * HALF, a.shape[2], a.shape[3]
    return pl.pallas_call(
        own_kernel,
        out_shape=(
            jax.ShapeDtypeStruct((rows * chunks * 2 * dates * pitch(dates), LANES), F32),
            jax.ShapeDtypeStruct((rows, chunks, dates, LANES), F32),
            jax.ShapeDtypeStruct((rows, chunks, 2, dates, LANES), F32),
            jax.ShapeDtypeStruct((2, chunks, rows, LANES), F32),
        ),
        in_specs=[vmem()] * 2,
        out_specs=[vmem()] * 4,
        scratch_shapes=[pltpu.VMEM((TURNS, 2, dates, LANES), F32)]
        + [pltpu.VMEM((rows * 2 * dates, band.shape[0]), BF16)] * group,
        compiler_params=params(),
        name="link_own",
    )(a, band)


def link_window(a, images, band, s, r, w, slots, paired):
    rows, chunks, dates, _ = r.shape
    scratch = [
        pltpu.VMEM((rows * 2 * (dates + SUB), band.shape[0]), BF16),
        pltpu.VMEM((slots, rows, chunks, 2, dates, LANES), F32),
        pltpu.VMEM((slots, rows, chunks, 2, SUB, LANES), F32),
        pltpu.VMEM((rows, chunks, SUB, LANES), F32),
        pltpu.VMEM((TURNS, 2, dates, LANES), F32),
        pltpu.VMEM((TURNS, 2, SUB, LANES), F32),
    ]
    if paired:
        scratch.append(pltpu.VMEM((3, 2, chunks, rows, LANES), F32))
    return pl.pallas_call(
        functools.partial(window_kernel, slots, paired),
        out_shape=jax.ShapeDtypeStruct((rows, chunks, 2, dates, LANES), F32),
        in_specs=[vmem()] * (5 + len(images)),
        out_specs=vmem(),
        scratch_shapes=scratch,
        compiler_params=params(),
        name="link_window",
    )(a, band, s, r, w, *images)


def swap(value, step):
    count = lax.axis_size("date")
    return lax.ppermute(value, "date", [(i, i ^ step) for i in range(count)])


def pick(cond, on_true, on_false):
    return jnp.where(cond, on_true, on_false)


def is_paired(x):
    return lax.axis_size("ms") == 2 and lax.axis_size("date") == 4 and x.shape[2] % (4 * SUB) == 0


def paired_windows(x):
    slabs = lax.axis_size("pix")
    block = block_of(lax.axis_index("date"), lax.axis_index("pix"))
    near = block < 2
    even = (block & 1) == 0
    lead = x.transpose(2, 0, 1, 3)
    rows = lead.shape[0] // 4
    reach = 2 * rows + HALF
    low, high = lead[:reach], lead[-reach:]
    own_pairs, far_pairs = [], []
    for date in range(4):
        for k in range(slabs):
            upper = block_of(date, k) < 2
            target = k - 1 if upper else k + 1
            inside = 0 <= target < slabs
            own_pairs.append((date * slabs + k, date * slabs + target if inside else (date ^ 1) * slabs + k))
            far_pairs.append(((date ^ 2) * slabs + (target if inside else k), date * slabs + k))
    outer = pick(near, lax.axis_index("pix") == 0, lax.axis_index("pix") == slabs - 1)
    top, bottom = lead[:HALF], lead[-HALF:]
    edge_own = lax.ppermute(pick(near, top, bottom), ("date", "pix"), own_pairs)
    edge_far = lax.ppermute(pick(near, bottom, top), ("date", "pix"), far_pairs)
    here = pick(near, low, high)
    far = swap(pick(near, high, low), 2)
    edge = jnp.concatenate([edge_own, edge_far], 2)
    edge = pick(outer, jnp.zeros_like(edge), edge)
    own = jnp.concatenate([here, far], 2)
    both = pick(near, jnp.concatenate([edge, own], 0), jnp.concatenate([own, edge], 0))
    tall = rows + 2 * HALF
    first, second = both[:tall], both[rows:]
    other = swap(pick(even, second, first), 1)
    return jnp.concatenate([pick(even, first, second), other], 2)


def plain_windows(x):
    count, slabs = lax.axis_size("date"), lax.axis_size("pix")
    me = lax.axis_index("date").astype(jnp.uint32)
    lead = x.transpose(2, 0, 1, 3)
    rows = lead.shape[0] // count
    tall = rows + 2 * HALF
    ups = [(k, k + 1) for k in range(slabs - 1)]
    downs = [(b, a) for a, b in ups]
    above = lax.ppermute(lead[-HALF:], "pix", ups)
    below = lax.ppermute(lead[:HALF], "pix", downs)
    padded = jnp.concatenate([above, lead, below], 0)

    def window(target):
        return lax.dynamic_slice_in_dim(padded, target * rows, tall, 0)

    parts = [window(me)] + [swap(window(me ^ step), step) for step in range(1, count)]
    return jnp.concatenate(parts, 2)


def earlier_windows(compressed, shift_by):
    stacks, count, slabs = lax.axis_size("ms"), lax.axis_size("date"), lax.axis_size("pix")
    rows = compressed.shape[1]
    reach = -(-HALF // rows)
    blocks = count * slabs

    def index(stack, block):
        k, d = divmod(block, count)
        return (stack * count + d) * slabs + k

    lead = compressed.transpose(1, 0, 2)
    parts = []
    for offset in range(-reach, reach + 1):
        low = max(0, -HALF - offset * rows)
        high = min(rows, rows + HALF - offset * rows)
        pairs = []
        for stack in range(stacks - shift_by):
            for block in range(blocks):
                target = block - offset
                if 0 <= target < blocks:
                    pairs.append((index(stack, block), index(stack + shift_by, target)))
        parts.append(lax.ppermute(lead[low:high], ("ms", "date", "pix"), pairs))
    return jnp.concatenate(parts, 0)


def assemble_kernel(offsets, *refs):
    date = lax.axis_index("date")
    block = block_of(date, lax.axis_index("pix"))
    pieces, (out_ref, mine_out_ref, whole_ref, mine_ref, sem) = refs[: len(offsets)], refs[len(offsets) :]
    own, rows = out_ref.shape[1], pieces[0].shape[2]
    copies = []
    for offset, piece in zip(offsets, pieces):
        row = pl.multiple_of((block ^ offset) * rows, rows)
        copy = pltpu.make_async_copy(
            piece.at[:, pl.ds(0, own)], out_ref.at[:, :, pl.ds(row, rows), :], sem.at[len(copies)]
        )
        copy.start()
        copies.append(copy)
        whole_ref[:, pl.ds(row, rows), :] = piece[:, own]
    width = mine_ref.shape[3]
    cols = whole_ref.shape[2]
    for c in range(2):
        rolled = pltpu.roll(whole_ref[c], lax.rem(cols - date * width, cols), 1)
        mine_ref[c, 0] = rolled[:, :width]
    copy = pltpu.make_async_copy(mine_ref, mine_out_ref, sem.at[len(copies)])
    copy.start()
    copies.append(copy)
    for copy in copies:
        copy.wait()


def assemble(pieces, offsets, count):
    _, own, rows, cols = pieces[0].shape
    own = own - 1
    return pl.pallas_call(
        functools.partial(assemble_kernel, offsets),
        out_shape=(
            jax.ShapeDtypeStruct((2, own, rows * count, cols), F32),
            jax.ShapeDtypeStruct((2, 1, rows * count, cols // count), F32),
        ),
        in_specs=[vmem()] * len(pieces),
        out_specs=[pl.BlockSpec(memory_space=pl.ANY)] * 2,
        scratch_shapes=[
            pltpu.VMEM((2, rows * count, cols), F32),
            pltpu.VMEM((2, 1, rows * count, cols // count), F32),
            pltpu.SemaphoreType.DMA((len(pieces) + 1,)),
        ],
        compiler_params=params(8),
        name="assemble",
    )(*pieces)


def scatter(blocks, compressed, me, paired):
    count = lax.axis_size("date")
    _, own, rows, cols = blocks[0].shape
    if paired:
        image = compressed[:, None]
        mine, far, sibling, far_sibling = blocks
        got = swap(jnp.concatenate([far, far_sibling, image], 1), 2)
        to_send = jnp.stack(
            [jnp.concatenate([sibling, image], 1), got[:, own:]], 0
        )
        near = swap(to_send, 1)
        pieces = [
            jnp.concatenate([mine, image], 1),
            jnp.concatenate([got[:, :own], got[:, 2 * own :]], 1),
            near[0],
            near[1],
        ]
        return assemble(pieces, (0, 2, 1, 3), count)
    out = jnp.zeros((2, own + 1, rows * count, cols), F32)
    for step in range(count):
        piece = jnp.concatenate([blocks[step], compressed[:, None]], 1)
        piece = swap(piece, step) if step else piece
        out = lax.dynamic_update_slice_in_dim(out, piece, (me ^ step) * rows, 2)
    width = cols // count
    return (out[:, :own], lax.dynamic_slice_in_dim(out[:, own:], me * width, width, 3))


def earlier_images(compressed):
    slabs = lax.axis_size("pix")
    blocks = 4 * slabs

    def index(stack, block):
        k, t = divmod(block, 4)
        return (stack * 4 + block_of(t, k)) * slabs + k

    def crossing(block):
        target = block + 1 if block & 1 else block - 1
        return target if 0 <= target < blocks else block

    def move(target_of):
        pairs = [
            (index(stack, block), index(1 - stack, target_of(block))) for stack in range(2) for block in range(blocks)
        ]
        return lax.ppermute(compressed, ("ms", "date", "pix"), pairs)

    return [move(lambda block: block), move(lambda block: block ^ 1), move(crossing)]


def body(slc_stack):
    count = lax.axis_size("date")
    rows = slc_stack.shape[2] // count
    paired = is_paired(slc_stack)
    a = paired_windows(slc_stack) if paired else plain_windows(slc_stack)
    cols = a.shape[3]
    chunks = cols // LANES
    a = a.reshape(a.shape[:3] + (chunks, LANES)).transpose(0, 1, 3, 2, 4)
    places = jnp.arange(cols, dtype=jnp.int32)
    band = (jnp.abs(places[:, None] - places[None, :]) <= HALF).astype(BF16)
    band = jnp.concatenate([band, band], 0)
    me = lax.axis_index("date").astype(jnp.uint32)
    a, me = lax.optimization_barrier((a, me))
    s, r, w, compressed = link_own(a, band)
    slots = min(3, lax.axis_size("ms") - 1)
    image = compressed.transpose(0, 2, 1, 3).reshape(2, rows, cols)
    if paired:
        images = earlier_images(compressed)
    else:
        z = jnp.stack([earlier_windows(image, shift_by) for shift_by in range(1, slots + 1)], 2)
        z = jnp.pad(z, ((0, 0), (0, 0), (0, SUB - slots), (0, 0)))
        images = [z.reshape(z.shape[:3] + (chunks, LANES)).transpose(0, 1, 3, 2, 4)]
    linked = link_window(a, images, band, s, r, w, slots, paired)
    own = slc_stack.shape[1]
    blocks = [
        linked[:, :, :, j * own : (j + 1) * own].transpose(2, 3, 0, 1, 4).reshape(2, own, rows, cols)
        for j in range(count)
    ]
    return scatter(blocks, image, me, paired)


def solution(mesh):
    in_specs = (P(None, ("ms", "date"), "pix", None),)
    out_specs = (P(None, ("ms", "date"), "pix", None), P(None, "ms", "pix", "date"))
    return jax.shard_map(body, mesh=mesh, in_specs=in_specs, out_specs=out_specs, check_vma=False)
```

```python
import functools
import itertools
import math

import jax
import jax.numpy as jnp
from jax import lax
from jax.experimental import pallas as pl
from jax.experimental.pallas import tpu as pltpu
from jax.sharding import PartitionSpec as P

HALF = 5
ITERS = 3
WIDTH = 2 * HALF + 1
AREA = float(WIDTH**2)
EPSILON = 1e-06
SUB = 8
LANES = 128
TURNS = 2
F32 = jnp.float32
BF16 = jnp.bfloat16


def row_sums(values, count):
    suffix = [None] * WIDTH
    running = values[WIDTH - 1]
    suffix[WIDTH - 1] = running
    for row in range(WIDTH - 2, -1, -1):
        running = running + values[row]
        suffix[row] = running
    out = [suffix[0]]
    prefix = None
    for row in range(1, count):
        term = values[WIDTH - 1 + row]
        prefix = term if prefix is None else prefix + term
        out.append(suffix[row] + prefix)
    return out


def put_split(x_ref, at, chunk, value):
    high = value.astype(BF16)
    low = (value - high.astype(F32)).astype(BF16)
    total = x_ref.shape[1] // 2
    x_ref[pl.ds(at, value.shape[0]), pl.ds(chunk * LANES, LANES)] = high
    x_ref[pl.ds(at, value.shape[0]), pl.ds(total + chunk * LANES, LANES)] = low


def products(x_ref, blocks, other, rows, chunks):
    for chunk in range(chunks):
        for place, (ref, first) in enumerate(blocks):
            at = pl.ds(first, SUB)
            real, imag = [], []
            for row in range(rows + 2 * HALF):
                left_real, left_imag = ref[row, 0, chunk, at, :], ref[row, 1, chunk, at, :]
                right_real, right_imag = other(row, chunk)
                real.append(left_real * right_real + left_imag * right_imag)
                imag.append(left_imag * right_real - left_real * right_imag)
            sums = zip(row_sums(real, rows), row_sums(imag, rows))
            for row, both in enumerate(sums):
                put_split(x_ref, (row * len(blocks) + place) * 2 * SUB, chunk, jnp.concatenate(both, 0))


def energies(x_ref, ref, rows, chunks, dates):
    step = math.gcd(dates, 2 * SUB)
    for chunk in range(chunks):
        for first in range(0, dates, step):
            at = pl.ds(first, step)
            values = []
            for row in range(rows + 2 * HALF):
                real, imag = ref[row, 0, chunk, at, :], ref[row, 1, chunk, at, :]
                values.append(real * real + imag * imag)
            for row, total in enumerate(row_sums(values, rows)):
                put_split(x_ref, row * dates + first, chunk, total)


def across(x_ref, size, band_ref, chunk):
    band = band_ref[:, pl.ds(chunk * LANES, LANES)]
    return jnp.dot(x_ref[0:size, :], band, preferred_element_type=F32)


def spread(ref, *place):
    return ref[place[:-1] + (pl.ds(place[-1], SUB, stride=0), slice(None))]


def pitch(dates):
    return dates if (dates // SUB) % 2 else dates + SUB


def accumulate(total, term):
    return term if total is None else total + term


def matvec(s_ref, v_ref, base, dates):
    blocks = dates // SUB
    real, imag = [None] * blocks, [None] * blocks
    for q in range(dates):
        v_real, v_imag = spread(v_ref, 0, q), spread(v_ref, 1, q)
        for b in range(blocks):
            at = q * pitch(dates) + b * SUB
            s_real = s_ref[pl.ds(base + at, SUB), :]
            s_imag = s_ref[pl.ds(base + dates * pitch(dates) + at, SUB), :]
            real[b] = accumulate(real[b], s_real * v_real - s_imag * v_imag)
            imag[b] = accumulate(imag[b], s_real * v_imag + s_imag * v_real)
    return jnp.concatenate(real, 0), jnp.concatenate(imag, 0)


def fill_and_apply(s_ref, v_ref, base, dates):
    blocks = dates // SUB
    real, imag = [None] * blocks, [None] * blocks
    half = dates * pitch(dates)
    for q in range(dates):
        v_real = spread(v_ref, 0, q)
        for b in range(blocks):
            at = pl.ds(base + q * pitch(dates) + b * SUB, SUB)
            at_imag = pl.ds(base + half + q * pitch(dates) + b * SUB, SUB)
            if b < q // SUB:
                turned = base + b * SUB * pitch(dates) + q
                s_real = s_ref[pl.ds(turned, SUB, stride=pitch(dates)), :]
                s_imag = -s_ref[pl.ds(turned + half, SUB, stride=pitch(dates)), :]
                s_ref[at, :] = s_real
                s_ref[at_imag, :] = s_imag
            else:
                s_real, s_imag = s_ref[at, :], s_ref[at_imag, :]
            real[b] = accumulate(real[b], s_real * v_real)
            imag[b] = accumulate(imag[b], s_imag * v_real)
    return jnp.concatenate(real, 0), jnp.concatenate(imag, 0)


def total_square(real, imag):
    return jnp.sum(real * real + imag * imag, axis=0, keepdims=True)


def each_row(rows, chunks, one_row):
    turns = math.gcd(rows, TURNS)
    for chunk in range(chunks):

        def together(step, carry, chunk=chunk):
            running = [one_row(chunk, step * turns + turn, turn) for turn in range(turns)]
            for _ in itertools.zip_longest(*running):
                pass
            return carry

        lax.fori_loop(0, rows // turns, together, 0)


def own_kernel(a_ref, band_ref, s_ref, r_ref, w_ref, comp_ref, v_ref, *x_refs):
    rows, chunks, dates, _ = r_ref.shape
    blocks = dates // SUB
    half = dates * pitch(dates)
    group = len(x_refs)

    for q_block in range(blocks):
        kept = [(a_ref, b * SUB) for b in range(q_block, blocks)]

        def one_group(turn, carry, q_block=q_block, kept=kept):
            for u in range(group):
                q = q_block * SUB + turn * group + u

                def other(row, chunk, q=q):
                    return spread(a_ref, row, 0, chunk, q), spread(a_ref, row, 1, chunk, q)

                products(x_refs[u], kept, other, rows, chunks)
                for chunk in range(chunks):
                    summed = across(x_refs[u], rows * len(kept) * 2 * SUB, band_ref, chunk)
                    for row in range(rows):
                        for place, (_, first) in enumerate(kept):
                            for c in range(2):
                                value = summed[((row * len(kept) + place) * 2 + c) * SUB :][:SUB]
                                at = (row * chunks + chunk) * 2 * half + c * half + q * pitch(dates) + first
                                s_ref[pl.ds(pl.multiple_of(at, SUB), SUB), :] = value
            return carry

        lax.fori_loop(0, SUB // group, one_group, 0)

    def one_row(chunk, row, turn):
        v = v_ref.at[turn]
        base = pl.multiple_of((row * chunks + chunk) * 2 * half, SUB)
        step = pitch(dates) + 1
        power = [s_ref[pl.ds(base + b * SUB * step, SUB, stride=step), :] for b in range(blocks)]
        scale = lax.rsqrt(jnp.concatenate(power, 0) / AREA + EPSILON)
        r_ref[row, chunk] = scale
        v[0] = scale
        for repeat in range(ITERS):
            if repeat == 0:
                real, imag = fill_and_apply(s_ref, v, base, dates)
            else:
                real, imag = matvec(s_ref, v, base, dates)
            real, imag = real * (scale / AREA), imag * (scale / AREA)
            if repeat == 0:
                w_ref[row, chunk, 0] = real
                w_ref[row, chunk, 1] = imag
            factor = lax.rsqrt(total_square(real, imag) / dates + EPSILON)
            real, imag = real * factor, imag * factor
            if repeat < ITERS - 1:
                v[0] = real * scale
                v[1] = imag * scale
            yield
        centre_real, centre_imag = a_ref[row + HALF, 0, chunk], a_ref[row + HALF, 1, chunk]
        root = math.sqrt(dates)
        comp_real = jnp.sum(real * centre_real + imag * centre_imag, axis=0, keepdims=True)
        comp_imag = jnp.sum(real * centre_imag - imag * centre_real, axis=0, keepdims=True)
        comp_ref[0, chunk, pl.ds(row, 1), :] = comp_real / root
        comp_ref[1, chunk, pl.ds(row, 1), :] = comp_imag / root

    each_row(rows, chunks, one_row)


def block_of(date, slab):
    return date ^ (2 * (slab & 1))


def fill_window(z_ref, images):
    centre_ref, sibling_ref, other_ref = images
    slab, slabs = lax.axis_index("pix"), lax.axis_size("pix")
    block = block_of(lax.axis_index("date"), slab)
    even = (block & 1) == 0
    known = lax.axis_index("ms") > 0
    inner = known & jnp.logical_not(((slab == 0) & (block == 0)) | ((slab == slabs - 1) & (block == 3)))
    sibling = jnp.where(known, sibling_ref[...], 0.0)
    other = jnp.where(inner, other_ref[...], 0.0)
    z_ref[0] = jnp.where(even, other, sibling)
    z_ref[1] = jnp.where(known, centre_ref[...], 0.0)
    z_ref[2] = jnp.where(even, sibling, other)


class Row:
    def __init__(self, z_ref, rows):
        self.z_ref, self.rows = z_ref, rows

    def __getitem__(self, index):
        row, c, chunk = index[:3]
        part, at = divmod(row - HALF + self.rows, self.rows)
        return spread(self.z_ref, part, c, chunk, at)


def window_kernel(slots, paired, *refs):
    a_ref, band_ref, s_ref, r_ref, w_ref = refs[:5]
    rows, chunks, dates, _ = r_ref.shape
    count = 3 if paired else 1
    images = refs[5 : 5 + count]
    out_ref, x_ref, m_ref, zz_ref, rz_ref, v_ref, vz_ref = refs[5 + count : 12 + count]
    blocks = dates // SUB
    half = dates * pitch(dates)
    if paired:
        fill_window(refs[12 + count], images)
        z = Row(refs[12 + count], rows)
    else:
        z = images[0]
        energies(x_ref, z, rows, chunks, SUB)
        for chunk in range(chunks):
            power = across(x_ref, rows * SUB, band_ref, chunk)
            rz_ref[:, chunk] = lax.rsqrt(power / AREA + EPSILON).reshape(rows, SUB, LANES)

    kept = [(a_ref, b * SUB) for b in range(blocks)] + [(z, 0)]
    for slot in range(slots):

        def other(row, chunk, slot=slot):
            if paired:
                return z[row, 0, chunk], z[row, 1, chunk]
            return spread(z, row, 0, chunk, slot), spread(z, row, 1, chunk, slot)

        products(x_ref, kept, other, rows, chunks)
        for chunk in range(chunks):
            summed = across(x_ref, rows * len(kept) * 2 * SUB, band_ref, chunk)
            for row in range(rows):
                for place, (_, first) in enumerate(kept):
                    for c in range(2):
                        value = summed[((row * len(kept) + place) * 2 + c) * SUB :][:SUB]
                        if place < blocks:
                            m_ref[slot, row, chunk, c, pl.ds(first, SUB), :] = value
                        else:
                            zz_ref[slot, row, chunk, c] = value
                            if paired and c == 0:
                                rz_ref[row, chunk] = lax.rsqrt(value / AREA + EPSILON)

    place = lax.broadcasted_iota(jnp.int32, (SUB, LANES), 0)

    def one_row(chunk, row, turn):
        v, vz = v_ref.at[turn], vz_ref.at[turn]
        base = pl.multiple_of((row * chunks + chunk) * 2 * half, SUB)
        scale = r_ref[row, chunk]
        scale_z = rz_ref[row, chunk]
        v[0] = scale
        v[1] = jnp.zeros_like(scale)
        vz[0] = scale_z
        vz[1] = jnp.zeros_like(scale_z)
        for repeat in range(ITERS):
            if repeat == 0:
                real, imag = w_ref[row, chunk, 0], w_ref[row, chunk, 1]
            else:
                real, imag = matvec(s_ref, v, base, dates)
                real, imag = real * (scale / AREA), imag * (scale / AREA)
            add_real, add_imag = jnp.zeros_like(real), jnp.zeros_like(imag)
            z_real, z_imag = jnp.zeros_like(scale_z), jnp.zeros_like(scale_z)
            old_real, old_imag = v[0], v[1]
            for slot in range(slots):
                v_real, v_imag = vz[0, pl.ds(slot, 1), :], vz[1, pl.ds(slot, 1), :]
                m_real, m_imag = m_ref[slot, row, chunk, 0], m_ref[slot, row, chunk, 1]
                add_real = add_real + m_real * v_real - m_imag * v_imag
                add_imag = add_imag + m_real * v_imag + m_imag * v_real
                sum_real = jnp.sum(m_real * old_real + m_imag * old_imag, axis=0, keepdims=True)
                sum_imag = jnp.sum(m_real * old_imag - m_imag * old_real, axis=0, keepdims=True)
                z_real = z_real + jnp.where(place == slot, sum_real, 0.0)
                z_imag = z_imag + jnp.where(place == slot, sum_imag, 0.0)
                zz_real, zz_imag = zz_ref[slot, row, chunk, 0], zz_ref[slot, row, chunk, 1]
                z_real = z_real + zz_real * v_real - zz_imag * v_imag
                z_imag = z_imag + zz_real * v_imag + zz_imag * v_real
            real = real + add_real * (scale / AREA)
            imag = imag + add_imag * (scale / AREA)
            z_real = jnp.where(place < slots, z_real * (scale_z / AREA), 0.0)
            z_imag = jnp.where(place < slots, z_imag * (scale_z / AREA), 0.0)
            square = total_square(real, imag) + total_square(z_real, z_imag)
            factor = lax.rsqrt(square / (slots + dates) + EPSILON)
            real, imag = real * factor, imag * factor
            if repeat < ITERS - 1:
                v[0] = real * scale
                v[1] = imag * scale
                vz[0] = z_real * factor * scale_z
                vz[1] = z_imag * factor * scale_z
            yield
        out_ref[row, chunk, 0] = real
        out_ref[row, chunk, 1] = imag

    each_row(rows, chunks, one_row)


def vmem():
    return pl.BlockSpec(memory_space=pltpu.VMEM)


def params(limit=24):
    return pltpu.CompilerParams(vmem_limit_bytes=limit * 2**20)


def link_own(a, band, group=8):
    rows, chunks, dates = a.shape[0] - 2 * HALF, a.shape[2], a.shape[3]
    return pl.pallas_call(
        own_kernel,
        out_shape=(
            jax.ShapeDtypeStruct((rows * chunks * 2 * dates * pitch(dates), LANES), F32),
            jax.ShapeDtypeStruct((rows, chunks, dates, LANES), F32),
            jax.ShapeDtypeStruct((rows, chunks, 2, dates, LANES), F32),
            jax.ShapeDtypeStruct((2, chunks, rows, LANES), F32),
        ),
        in_specs=[vmem()] * 2,
        out_specs=[vmem()] * 4,
        scratch_shapes=[pltpu.VMEM((TURNS, 2, dates, LANES), F32)]
        + [pltpu.VMEM((rows * 2 * dates, band.shape[0]), BF16)] * group,
        compiler_params=params(),
        name="link_own",
    )(a, band)


def link_window(a, images, band, s, r, w, slots, paired):
    rows, chunks, dates, _ = r.shape
    scratch = [
        pltpu.VMEM((rows * 2 * (dates + SUB), band.shape[0]), BF16),
        pltpu.VMEM((slots, rows, chunks, 2, dates, LANES), F32),
        pltpu.VMEM((slots, rows, chunks, 2, SUB, LANES), F32),
        pltpu.VMEM((rows, chunks, SUB, LANES), F32),
        pltpu.VMEM((TURNS, 2, dates, LANES), F32),
        pltpu.VMEM((TURNS, 2, SUB, LANES), F32),
    ]
    if paired:
        scratch.append(pltpu.VMEM((3, 2, chunks, rows, LANES), F32))
    return pl.pallas_call(
        functools.partial(window_kernel, slots, paired),
        out_shape=jax.ShapeDtypeStruct((rows, chunks, 2, dates, LANES), F32),
        in_specs=[vmem()] * (5 + len(images)),
        out_specs=vmem(),
        scratch_shapes=scratch,
        compiler_params=params(),
        name="link_window",
    )(a, band, s, r, w, *images)


def swap(value, step):
    count = lax.axis_size("date")
    return lax.ppermute(value, "date", [(i, i ^ step) for i in range(count)])


def pick(cond, on_true, on_false):
    return jnp.where(cond, on_true, on_false)


def is_paired(x):
    return lax.axis_size("ms") == 2 and lax.axis_size("date") == 4 and x.shape[2] % (4 * SUB) == 0


def paired_windows(x):
    slabs = lax.axis_size("pix")
    block = block_of(lax.axis_index("date"), lax.axis_index("pix"))
    near = block < 2
    even = (block & 1) == 0
    lead = x.transpose(2, 0, 1, 3)
    rows = lead.shape[0] // 4
    reach = 2 * rows + HALF
    low, high = lead[:reach], lead[-reach:]
    own_pairs, far_pairs = [], []
    for date in range(4):
        for k in range(slabs):
            upper = block_of(date, k) < 2
            target = k - 1 if upper else k + 1
            inside = 0 <= target < slabs
            own_pairs.append((date * slabs + k, date * slabs + target if inside else (date ^ 1) * slabs + k))
            far_pairs.append(((date ^ 2) * slabs + (target if inside else k), date * slabs + k))
    outer = pick(near, lax.axis_index("pix") == 0, lax.axis_index("pix") == slabs - 1)
    top, bottom = lead[:HALF], lead[-HALF:]
    edge_own = lax.ppermute(pick(near, top, bottom), ("date", "pix"), own_pairs)
    edge_far = lax.ppermute(pick(near, bottom, top), ("date", "pix"), far_pairs)
    here = pick(near, low, high)
    far = swap(pick(near, high, low), 2)
    edge = jnp.concatenate([edge_own, edge_far], 2)
    edge = pick(outer, jnp.zeros_like(edge), edge)
    own = jnp.concatenate([here, far], 2)
    both = pick(near, jnp.concatenate([edge, own], 0), jnp.concatenate([own, edge], 0))
    tall = rows + 2 * HALF
    first, second = both[:tall], both[rows:]
    other = swap(pick(even, second, first), 1)
    return jnp.concatenate([pick(even, first, second), other], 2)


def plain_windows(x):
    count, slabs = lax.axis_size("date"), lax.axis_size("pix")
    me = lax.axis_index("date").astype(jnp.uint32)
    lead = x.transpose(2, 0, 1, 3)
    rows = lead.shape[0] // count
    tall = rows + 2 * HALF
    ups = [(k, k + 1) for k in range(slabs - 1)]
    downs = [(b, a) for a, b in ups]
    above = lax.ppermute(lead[-HALF:], "pix", ups)
    below = lax.ppermute(lead[:HALF], "pix", downs)
    padded = jnp.concatenate([above, lead, below], 0)

    def window(target):
        return lax.dynamic_slice_in_dim(padded, target * rows, tall, 0)

    parts = [window(me)] + [swap(window(me ^ step), step) for step in range(1, count)]
    return jnp.concatenate(parts, 2)


def earlier_windows(compressed, shift_by):
    stacks, count, slabs = lax.axis_size("ms"), lax.axis_size("date"), lax.axis_size("pix")
    rows = compressed.shape[1]
    reach = -(-HALF // rows)
    blocks = count * slabs

    def index(stack, block):
        k, d = divmod(block, count)
        return (stack * count + d) * slabs + k

    lead = compressed.transpose(1, 0, 2)
    parts = []
    for offset in range(-reach, reach + 1):
        low = max(0, -HALF - offset * rows)
        high = min(rows, rows + HALF - offset * rows)
        pairs = []
        for stack in range(stacks - shift_by):
            for block in range(blocks):
                target = block - offset
                if 0 <= target < blocks:
                    pairs.append((index(stack, block), index(stack + shift_by, target)))
        parts.append(lax.ppermute(lead[low:high], ("ms", "date", "pix"), pairs))
    return jnp.concatenate(parts, 0)


def assemble_kernel(offsets, *refs):
    date = lax.axis_index("date")
    block = block_of(date, lax.axis_index("pix"))
    pieces, (out_ref, mine_out_ref, whole_ref, mine_ref, sem) = refs[: len(offsets)], refs[len(offsets) :]
    own, rows = out_ref.shape[1], pieces[0].shape[2]
    copies = []
    for offset, piece in zip(offsets, pieces):
        row = pl.multiple_of((block ^ offset) * rows, rows)
        copy = pltpu.make_async_copy(
            piece.at[:, pl.ds(0, own)], out_ref.at[:, :, pl.ds(row, rows), :], sem.at[len(copies)]
        )
        copy.start()
        copies.append(copy)
        whole_ref[:, pl.ds(row, rows), :] = piece[:, own]
    width = mine_ref.shape[3]
    cols = whole_ref.shape[2]
    for c in range(2):
        rolled = pltpu.roll(whole_ref[c], lax.rem(cols - date * width, cols), 1)
        mine_ref[c, 0] = rolled[:, :width]
    copy = pltpu.make_async_copy(mine_ref, mine_out_ref, sem.at[len(copies)])
    copy.start()
    copies.append(copy)
    for copy in copies:
        copy.wait()


def assemble(pieces, offsets, count):
    _, own, rows, cols = pieces[0].shape
    own = own - 1
    return pl.pallas_call(
        functools.partial(assemble_kernel, offsets),
        out_shape=(
            jax.ShapeDtypeStruct((2, own, rows * count, cols), F32),
            jax.ShapeDtypeStruct((2, 1, rows * count, cols // count), F32),
        ),
        in_specs=[vmem()] * len(pieces),
        out_specs=[pl.BlockSpec(memory_space=pl.ANY)] * 2,
        scratch_shapes=[
            pltpu.VMEM((2, rows * count, cols), F32),
            pltpu.VMEM((2, 1, rows * count, cols // count), F32),
            pltpu.SemaphoreType.DMA((len(pieces) + 1,)),
        ],
        compiler_params=params(8),
        name="assemble",
    )(*pieces)


def scatter(blocks, compressed, me, paired):
    count = lax.axis_size("date")
    _, own, rows, cols = blocks[0].shape
    if paired:
        image = compressed[:, None]
        mine, far, sibling, far_sibling = blocks
        got = swap(jnp.concatenate([far, far_sibling, image], 1), 2)
        to_send = jnp.stack(
            [jnp.concatenate([sibling, image], 1), got[:, own:]], 0
        )
        near = swap(to_send, 1)
        pieces = [
            jnp.concatenate([mine, image], 1),
            jnp.concatenate([got[:, :own], got[:, 2 * own :]], 1),
            near[0],
            near[1],
        ]
        return assemble(pieces, (0, 2, 1, 3), count)
    out = jnp.zeros((2, own + 1, rows * count, cols), F32)
    for step in range(count):
        piece = jnp.concatenate([blocks[step], compressed[:, None]], 1)
        piece = swap(piece, step) if step else piece
        out = lax.dynamic_update_slice_in_dim(out, piece, (me ^ step) * rows, 2)
    width = cols // count
    return (out[:, :own], lax.dynamic_slice_in_dim(out[:, own:], me * width, width, 3))


def earlier_images(compressed):
    slabs = lax.axis_size("pix")
    blocks = 4 * slabs

    def index(stack, block):
        k, t = divmod(block, 4)
        return (stack * 4 + block_of(t, k)) * slabs + k

    def crossing(block):
        target = block + 1 if block & 1 else block - 1
        return target if 0 <= target < blocks else block

    def move(target_of):
        pairs = [
            (index(stack, block), index(1 - stack, target_of(block))) for stack in range(2) for block in range(blocks)
        ]
        return lax.ppermute(compressed, ("ms", "date", "pix"), pairs)

    centre, other = move(lambda block: block), move(crossing)
    return [centre, swap(centre, 1), other]


def body(slc_stack):
    count = lax.axis_size("date")
    rows = slc_stack.shape[2] // count
    paired = is_paired(slc_stack)
    a = paired_windows(slc_stack) if paired else plain_windows(slc_stack)
    cols = a.shape[3]
    chunks = cols // LANES
    a = a.reshape(a.shape[:3] + (chunks, LANES)).transpose(0, 1, 3, 2, 4)
    places = jnp.arange(cols, dtype=jnp.int32)
    band = (jnp.abs(places[:, None] - places[None, :]) <= HALF).astype(BF16)
    band = jnp.concatenate([band, band], 0)
    me = lax.axis_index("date").astype(jnp.uint32)
    a, me = lax.optimization_barrier((a, me))
    s, r, w, compressed = link_own(a, band)
    slots = min(3, lax.axis_size("ms") - 1)
    image = compressed.transpose(0, 2, 1, 3).reshape(2, rows, cols)
    if paired:
        images = earlier_images(compressed)
    else:
        z = jnp.stack([earlier_windows(image, shift_by) for shift_by in range(1, slots + 1)], 2)
        z = jnp.pad(z, ((0, 0), (0, 0), (0, SUB - slots), (0, 0)))
        images = [z.reshape(z.shape[:3] + (chunks, LANES)).transpose(0, 1, 3, 2, 4)]
    linked = link_window(a, images, band, s, r, w, slots, paired)
    own = slc_stack.shape[1]
    blocks = [
        linked[:, :, :, j * own : (j + 1) * own].transpose(2, 3, 0, 1, 4).reshape(2, own, rows, cols)
        for j in range(count)
    ]
    return scatter(blocks, image, me, paired)


def solution(mesh):
    in_specs = (P(None, ("ms", "date"), "pix", None),)
    out_specs = (P(None, ("ms", "date"), "pix", None), P(None, "ms", "pix", "date"))
    return jax.shard_map(body, mesh=mesh, in_specs=in_specs, out_specs=out_specs, check_vma=False)
```
